32 devices in a mesh: seg: 4 (over y, x), bin: 8 (over z, core).
Axes of the slice: x: 2, y: 2, z: 4, core: 2. Of those that a mesh axis runs over, the one named last changes fastest.
Arguments:
- coverage_lanes: bfloat16 [256, 128, 128], P(('seg', 'bin')), may hold values from 4 to 64
- target_blocks: int32 [256], P(('seg', 'bin')), may hold values from 0 to 7, as said below
- valid_bins: int32 [256], P(('seg', 'bin')), may hold values from 1 to 128
- panel_mean: float32 [32768], P(('seg', 'bin')), may hold values from 3.5 to 5
- components: float32 [256, 32768], P(None, ('seg', 'bin')), as said below
- kernels: float32 [3, 33, 32768], P(None, None, ('seg', 'bin')), may hold values from 0 to 0.08
- chrom_starts: int32 [24], replicated, may hold values from 0 to 32767, as said below
Outputs:
- coefficients: float32 [128, 256], replicated
- smoothed: float32 [128, 32768], P(None, ('seg', 'bin'))
- bridge: float32 [128, 32768], P(None, ('seg', 'bin'))
The draws below stay inside these ranges and needn't reach their ends.
Inputs may be any that keep to these rules, and one draw needn't show every extreme that they name: target_blocks names one of the owner's 8 blocks; slot r of a device goes to the owner given by r // 1 within the device's stretch. `chrom_starts`: strictly rising chromosome starts, the first is 0 and the last is 32767. panel-of-normals components.
All inputs are finite; a program needn't handle non-finite values.
Results may differ from the reference program's by a relative error of at most 0.0003.
Values may be sent and summed in bfloat16 or wider, within the bound.
A program may use at most 192 MiB of HBM per device.

```python
import math
import jax
import jax.numpy as jnp
from jax import lax

SAMPLES = 128
COMPONENTS = 256
TAPS = 33
NCONV = 3
BLOCK = 128
NCHROM = 24
BLK_DEV = 8
CAP = 1
HALF = 16
BINS = 32768
LANE_SLOTS = 256
N_SEG = 4
N_BIN = 8


def draw_target_blocks(key, part):
    picks = jax.random.randint(jax.random.fold_in(key, 11), (LANE_SLOTS,), 0, BLK_DEV, dtype=jnp.int32)
    picks = picks.at[0].set(BLK_DEV - 1)
    return picks.at[1].set(0)


def draw_valid_bins(key, part):
    picks = jax.random.randint(jax.random.fold_in(key, 23), (LANE_SLOTS,), 1, BLOCK + 1, dtype=jnp.int32)
    picks = picks.at[0].set(BLOCK)
    return picks.at[1].set(1)


def draw_components(key, part):
    key_noise = jax.random.fold_in(key, 37)
    noise = jax.random.normal(key_noise, (COMPONENTS, BINS), jnp.float32)
    return noise * (1.0 / math.sqrt(BINS))


def draw_chrom_starts(key, part):
    shuffled = jax.random.permutation(jax.random.fold_in(key, 53), BINS - 2)[:NCHROM - 2] + 1
    inner = jnp.sort(shuffled).astype(jnp.int32)
    return jnp.concatenate([jnp.zeros((1,), jnp.int32), inner, jnp.full((1,), BINS - 1, jnp.int32)])


def level_of(stream_key, extent, pieces, least, largest):
    level = 1.0
    for axis_at, blocks in pieces:
        draws = jax.random.uniform(jax.random.fold_in(jax.random.fold_in(stream_key, 6), axis_at), (blocks,), jnp.float32, least / len(pieces), largest / len(pieces))
        level = level * jnp.repeat(jnp.exp(draws), extent[axis_at] // blocks).reshape((-1,) + (1,) * (len(extent) - 1 - axis_at))
    return level


def setup_inputs(seed: int = 0) -> dict:
    seeds = jax.random.split(jax.random.key(seed), 8)
    return {
        "coverage_lanes": jnp.clip(jnp.exp(math.log(64.0) - 2.7725887 * jax.random.uniform(seeds[0], (LANE_SLOTS, SAMPLES, BLOCK), jnp.float32) ** level_of(seeds[0], (LANE_SLOTS, SAMPLES, BLOCK), ((0, 32),), -0.2, 0.2)), 4.0, 64.0).astype(jnp.bfloat16),
        "target_blocks": draw_target_blocks(jax.random.fold_in(seeds[7], 71), 0),
        "valid_bins": draw_valid_bins(jax.random.fold_in(seeds[7], 71), 0),
        "panel_mean": jnp.clip(3.5 + 1.5 * jax.random.uniform(seeds[3], (BINS,), jnp.float32) ** level_of(seeds[3], (BINS,), ((0, 32),), -0.2, 0.2), 3.5, 5.0),
        "components": draw_components(jax.random.fold_in(seeds[7], 71), 0),
        "kernels": jnp.clip(0.08 * jax.random.uniform(seeds[5], (NCONV, TAPS, BINS), jnp.float32) ** level_of(seeds[5], (NCONV, TAPS, BINS), ((2, 32),), -0.2, 0.2), 0.0, 0.08),
        "chrom_starts": draw_chrom_starts(jax.random.fold_in(seeds[7], 71), 0),
    }


def chrom_labels(chrom_starts, first_bin, count, total_bins):
    positions = first_bin + jnp.arange(count, dtype=jnp.int32)
    covered = lax.optimization_barrier(jnp.sum((chrom_starts[:, None] <= positions[None, :]).astype(jnp.int32), axis=0)) - 1
    return jnp.where(positions >= total_bins, chrom_starts.shape[0], covered)

def smooth_once(padded, tap_weights, labels, out_width):
    half_taps = (tap_weights.shape[0] - 1) // 2
    centre = labels[half_taps:half_taps + out_width]
    result = jnp.zeros((padded.shape[0], out_width), jnp.float32)
    for tap_index in range(tap_weights.shape[0]):
        weight = tap_weights[tap_index] * (labels[tap_index:tap_index + out_width] == centre).astype(jnp.float32)
        result = result + weight[None, :] * padded[:, tap_index:tap_index + out_width]
    return result

def reference(coverage_lanes, target_blocks, valid_bins, panel_mean, components, kernels, chrom_starts):
    per_device = N_BIN * CAP
    slot_ids = jnp.arange(LANE_SLOTS, dtype=jnp.int32)
    sender = slot_ids // per_device
    owner = sender // N_BIN * N_BIN + slot_ids % per_device // CAP
    block_ids = (owner * BLK_DEV + target_blocks).astype(jnp.int32)
    keep_mask = (jnp.arange(BLOCK, dtype=jnp.int32)[None, :] < valid_bins[:, None]).astype(jnp.bfloat16)

    def add_device(device_index, gathered):
        start = (device_index * per_device).astype(jnp.int32)
        rows = lax.dynamic_slice_in_dim(coverage_lanes, start, per_device, 0)
        masks = lax.dynamic_slice_in_dim(keep_mask, start, per_device, 0)
        places = lax.dynamic_slice_in_dim(block_ids, start, per_device, 0)
        masked = (rows * masks[:, None, :]).astype(jnp.float32)
        return gathered.at[places].add(masked)
    gathered = lax.fori_loop(0, N_SEG * N_BIN, add_device, jnp.zeros((BINS // BLOCK, SAMPLES, BLOCK), jnp.float32))
    coverage = jnp.transpose(gathered, (1, 0, 2)).reshape(SAMPLES, BINS)
    log_ratio = jnp.log(coverage + 1.0) - panel_mean[None, :]
    coefficients = jnp.dot(log_ratio, components.T, precision=lax.Precision.HIGHEST, preferred_element_type=jnp.float32)
    signal = log_ratio - jnp.dot(coefficients, components, precision=lax.Precision.HIGHEST, preferred_element_type=jnp.float32)
    labels = chrom_labels(chrom_starts, -HALF, BINS + 2 * HALF, BINS)
    smoothed = signal
    for layer_index in range(NCONV):
        padded = jnp.pad(smoothed, ((0, 0), (HALF, HALF)))
        smoothed = smooth_once(padded, kernels[layer_index], labels, BINS)
    mean_level = lax.optimization_barrier(jnp.sum(smoothed, axis=1)) / BINS
    bridge = jnp.cumsum(smoothed - mean_level[:, None], axis=1) * (1.0 / math.sqrt(BINS))
    return (coefficients, smoothed, bridge)
```

```python
import functools
import math

import jax
import jax.numpy as jnp
from jax import lax
from jax.experimental import pallas as pl
from jax.experimental.pallas import tpu as pltpu
from jax.sharding import PartitionSpec as P

MESH = pl.DeviceIdType.MESH
F32, BF16 = jnp.float32, jnp.bfloat16
LANES = 128


def split(x):
    high = x.astype(BF16)
    return high, (x - high.astype(F32)).astype(BF16)


def mm(a, b, contract=(1, 0)):
    return lax.dot_general(
        a, b, (((contract[0],), (contract[1],)), ((), ())), preferred_element_type=F32
    )


def iota(shape, dim):
    return lax.broadcasted_iota(jnp.int32, shape, dim)


def wait_bytes(ref, sem):
    pltpu.make_async_copy(ref, ref, sem).wait()


def body(
    nseg, nb, targets_h, valid_h, starts_h, lanes_h, panel_h, comp, kern,
    coef_o, smooth_o, skh, skl, level_o,
    targets, valid, starts, panel,
    recv_l, kx, taps, lrx, kh, kl, lh, ll, ah, al, bh, bl,
    weights, part, gathered, c2, sums_l, sums_k, kout, kin, ssem, rsem, lsem,
):
    ndev = nseg * nb
    seg, place = lax.axis_index("seg"), lax.axis_index("bin")
    me = seg * nb + place
    samples, bin_dev = smooth_o.shape
    comps = kx.shape[0]
    blocks = bin_dev // LANES
    total_bins = bin_dev * ndev
    first = me * bin_dev
    ntaps = kern.shape[1]
    half = (ntaps - 1) // 2
    group = samples // 2

    def dev(flat):
        return (lax.div(flat, nb), lax.rem(flat, nb))

    def remote(src, dst, which, device):
        return pltpu.make_async_remote_copy(
            src_ref=src, dst_ref=dst, send_sem=ssem.at[which], recv_sem=rsem.at[which],
            device_id=device, device_id_type=MESH,
        )

    barrier = pltpu.get_barrier_semaphore()

    def each(start, stop, do):
        if stop - start <= 16:
            for hop in range(start, stop):
                do(hop)
        else:
            pl.loop(start, stop)(do)

    def bin_peer(hop):
        return (seg, lax.rem(place + hop, nb))

    def others(do):
        for turn in range(nseg - 1, -1, -1):
            other = lax.rem(seg + turn, nseg)
            each(0 if turn else 1, nb, lambda hop: do((other, lax.rem(place + hop, nb))))

    right, left = dev(lax.rem(me + 1, ndev)), dev(lax.rem(me + ndev - 1, ndev))

    others(lambda device: pl.semaphore_signal(
        barrier, inc=1, device_id=device, device_id_type=MESH
    ))

    fetched = [
        pltpu.make_async_copy(src, dst, lsem.at[i])
        for i, (src, dst) in enumerate(
            (
                (starts_h, starts), (panel_h, panel),
                (kern, taps.at[:, :, pl.ds(LANES, bin_dev)]),
                (comp, kx.at[:, pl.ds(LANES, bin_dev)]),
                (targets_h, targets.at[place]), (valid_h, valid.at[place]),
                (lanes_h.at[place, pl.ds(0, group), :], recv_l.at[0, place]),
                (lanes_h.at[place, pl.ds(group, group), :], recv_l.at[1, place]),
            )
        )
    ]
    for copy in fetched:
        copy.start()
    own_s, own_p, own_t, own_k = fetched[:4]

    pl.semaphore_wait(barrier, ndev - 1)

    def mark(hop):
        to = bin_peer(hop)
        remote(targets_h, targets.at[place], 2, to).start()
        remote(valid_h, valid.at[place], 3, to).start()

    each(1, nb, mark)
    for h in range(2):

        def exchange(hop, h=h):
            to = bin_peer(hop)
            remote(
                lanes_h.at[to[1], pl.ds(h * group, group), :], recv_l.at[h, place], h, to
            ).start()

        each(1, nb, exchange)
    low, high = pl.ds(0, LANES), pl.ds(bin_dev + LANES, LANES)
    head, tail = pl.ds(0, LANES), pl.ds(bin_dev - LANES, LANES)
    halos = [
        remote(kern.at[pl.ds(0, 2), :, tail], taps.at[pl.ds(0, 2), :, low], 4, right),
        remote(kern.at[pl.ds(0, 2), :, head], taps.at[pl.ds(0, 2), :, high], 5, left),
        remote(kout.at[0], kin.at[0], 6, right),
        remote(kout.at[1], kin.at[1], 7, left),
    ]
    for copy in halos[:2]:
        copy.start()
    own_k.wait()
    lower_half = iota((LANES, LANES), 1) < LANES // 2
    first_block, last_block = pl.ds(LANES, LANES), pl.ds(bin_dev, LANES)
    kout[0] = jnp.where(
        lower_half, pltpu.roll(kx[LANES:, last_block], LANES // 2, 1), kx[:LANES, last_block]
    )
    kout[1] = jnp.where(
        lower_half, kx[:LANES, first_block], pltpu.roll(kx[LANES:, first_block], LANES // 2, 1)
    )
    for copy in halos[2:]:
        copy.start()

    own = pl.ds(LANES, bin_dev)
    for ref in (ah, al, bh, bl):
        ref[:, pl.ds(bin_dev + LANES, LANES)] = jnp.zeros((comps, LANES), BF16)
    kh[:, own], kl[:, own] = split(kx[:, own])

    own_s.wait()
    own_t.wait()

    def band(layer, m, offset, top):
        if offset == LANES:
            columns = pl.ds(pl.multiple_of((m + 1) * LANES, LANES), LANES)
            upper = taps[layer, : 2 * half, columns]
            last = taps[layer, 2 * half : ntaps, columns]
        else:
            columns = pl.ds(pl.multiple_of(m * LANES, LANES), 2 * LANES)
            upper = taps[layer, : 2 * half, columns]
            last = taps[layer, 2 * half : ntaps, columns]
        last = jnp.broadcast_to(last, (8, last.shape[1]))
        last = jnp.where(iota(last.shape, 0) == 0, last, 0.0)
        rows = jnp.concatenate([upper, last], axis=0)
        if offset != LANES:
            rows = pltpu.roll(rows, 2 * LANES - offset, 1)[:, :LANES]
        position = first - LANES + offset + m * LANES + iota((8, LANES), 1)
        lower = jnp.full((8, LANES), total_bins, jnp.int32)
        upto = jnp.where(position < total_bins, total_bins, -1)
        count = starts.shape[0]
        for k in range(count):
            lower = jnp.where(starts[k] <= position, starts[k], lower)
        for k in range(count - 1, -1, -1):
            upto = jnp.where(starts[k] > position, starts[k], upto)
        tall = rows.shape[0]
        source = position[:1] + iota((tall, LANES), 0) - half
        inside = (source >= lower[:1]) & (source < upto[:1])
        rows = jnp.where(inside, rows, 0.0)
        lane = iota((1, LANES), 1)
        step = 1
        while step < LANES:
            if step < 8:
                moved = pltpu.roll(rows, step, 0)
                still = rows
            else:
                pad = jnp.zeros((step, LANES), F32)
                moved = jnp.concatenate([pad, rows], axis=0)
                still = jnp.concatenate([rows, pad], axis=0)
            chosen = jnp.broadcast_to((lane & step) != 0, moved.shape)
            rows = jnp.where(chosen, moved, still)
            step *= 2
        rest = 2 * LANES - rows.shape[0] - top
        pieces = [rows, jnp.zeros((rest, LANES), F32)]
        if top:
            pieces = [jnp.zeros((top, LANES), F32)] + pieces
        return split(jnp.concatenate(pieces, axis=0))

    plan = (
        (0, LANES - 2 * half, LANES - 3 * half, 0, blocks + 1),
        (1, LANES - half, 0, blocks + 1, blocks + 1),
        (2, LANES, 0, 2 * blocks + 2, blocks),
    )

    def build(layer, offset, top, base, m):
        w_high, w_low = band(layer, m, offset, top)
        weights[base + m, :, :LANES] = w_high
        weights[base + m, :, LANES:] = w_low

    for layer, offset, top, base, many in plan:
        inner = (0, many) if offset == LANES else (1, many - 1)

        @pl.loop(*inner)
        def _(m, layer=layer, offset=offset, top=top, base=base):
            build(layer, offset, top, base, m)

    def smooth_pass(src_high, src_low, m, base):
        window = pl.ds(m * LANES, 2 * LANES)
        both = mm(src_high[:, window], weights[base + m])
        return both[:, :LANES] + both[:, LANES:] + mm(
            src_low[:, window], weights[base + m, :, :LANES]
        )

    def smooth_first(src, mid, rows, which):
        for m in which:
            out = split(smooth_pass(src[0], src[1], m, plan[0][3]))
            for ref, value in zip(mid, out):
                ref[:rows, pl.ds(m * LANES, LANES)] = value

    def smooth_rest(mid, end, rows, store):
        for m in range(blocks + 1):
            out = split(
                smooth_pass(mid[0].at[:rows], mid[1].at[:rows], m, plan[1][3])
            )
            for ref, value in zip(end, out):
                ref[:rows, pl.ds(m * LANES, LANES)] = value
        total = jnp.zeros((rows, LANES), F32)
        for m in range(blocks):
            out = smooth_pass(end[0].at[:rows], end[1].at[:rows], m, plan[2][3])
            store(m, out)
            total = total + out
        return jnp.sum(total, axis=1, keepdims=True)

    eye = iota((LANES, LANES), 0) == iota((LANES, LANES), 1)

    def as_row(column):
        return jnp.sum(jnp.where(eye, column, 0.0), axis=0, keepdims=True)

    smooth_first((kh, kl), (ah, al), comps, range(1, blocks))

    def store_k(m, out):
        window = pl.ds(m * LANES, LANES)
        skh[:, window], skl[:, window] = split(out)

    rows = max(8, part.shape[0] // ndev)
    chunks = part.shape[0] // rows
    stride = ndev // chunks
    mine, side = lax.div(me, 2 * stride), lax.rem(lax.div(me, stride), 2)
    per_half = chunks // 2

    def chunk(h, j):
        return pl.ds(pl.multiple_of((h * per_half + j) * rows, 8), rows)

    def owner_of(h):
        mine_here = side == h
        if stride > 1:
            mine_here = jnp.logical_and(mine_here, lax.rem(me, stride) == 0)
        return mine_here

    own_p.wait()
    for copy in fetched[4:]:
        copy.wait()
    wait_bytes(targets.at[pl.ds(0, nb - 1)], rsem.at[2])
    wait_bytes(valid.at[pl.ds(0, nb - 1)], rsem.at[3])
    lane = iota((group, LANES), 1)
    near = []

    def reduce_half(h):
        mine_rows = pl.ds(h * group, group)
        wait_bytes(recv_l.at[h, pl.ds(0, nb - 1)], rsem.at[h])
        for b in range(blocks):

            def add(r, acc):
                upto = jnp.where(targets[r, place] == b, valid[r, place], 0)
                return acc + jnp.where(lane < upto, recv_l[h, r].astype(F32), 0.0)

            cover = lax.fori_loop(0, nb, add, jnp.zeros((group, LANES), F32), unroll=nb <= 8)
            value = jnp.log(cover + 1.0) - panel[:, pl.ds(b * LANES, LANES)]
            window = pl.ds((b + 1) * LANES, LANES)
            lrx[mine_rows, window] = value
            lh[mine_rows, window], ll[mine_rows, window] = split(value)
        terms = (
            mm(lh[mine_rows, own], kh[:, own], (1, 1))
            + mm(ll[mine_rows, own], kh[:, own], (1, 1))
            + mm(lh[mine_rows, own], kl[:, own], (1, 1))
        )
        for c in range(comps // LANES):
            part[pl.ds(h * per_half * rows + c * group, group), :] = terms[
                :, c * LANES : (c + 1) * LANES
            ]

        def spread(hop):
            j = lax.rem(mine + hop, per_half)
            flat = (2 * j + h) * stride
            pl.when(flat != me)(remote(
                part.at[chunk(h, j)], gathered.at[me], 12 + h, dev(flat)
            ).start)

        each(0, per_half, spread)
        pair = [
            remote(lrx.at[mine_rows, pl.ds(bin_dev, LANES)], lrx.at[mine_rows, low],
                   8 + 2 * h, right),
            remote(lrx.at[mine_rows, pl.ds(LANES, LANES)], lrx.at[mine_rows, high],
                   9 + 2 * h, left),
        ]
        for copy in pair:
            copy.start()
        near.extend(pair)

    reduce_half(0)
    reduce_half(1)

    halos[0].wait_recv()
    halos[1].wait_recv()
    for layer, offset, top, base, many in plan[:2]:
        for m in (0, many - 1):
            build(layer, offset, top, base, m)
    halos[2].wait_recv()
    halos[3].wait_recv()
    for at, edge in enumerate((low, high)):
        kh[:LANES, edge], kl[:LANES, edge] = split(kin[at])
        kh[LANES:, edge], kl[LANES:, edge] = split(pltpu.roll(kin[at], LANES // 2, 1))
    smooth_first((kh, kl), (ah, al), comps, (0, blocks))
    k_total = smooth_rest((ah, al), (bh, bl), comps, store_k)
    sums_k[me] = jnp.concatenate(
        [as_row(k_total[c * LANES : (c + 1) * LANES]) for c in range(comps // LANES)], axis=0
    )
    others(lambda device: remote(sums_k.at[me], sums_k.at[me], 17, device).start())

    def add_and_return(h):
        gathered[me] = part[chunk(h, mine), :]
        wait_bytes(gathered.at[pl.ds(0, ndev - 1)], rsem.at[12 + h])
        c2[chunk(h, mine), :] = jnp.sum(gathered[...], axis=0)
        others(lambda device: remote(
            c2.at[chunk(h, mine)], c2.at[chunk(h, mine)], 14 + h, device
        ).start())

    pl.when(owner_of(0))(lambda: add_and_return(0))

    for copy in near:
        copy.wait_recv()
    for edge in (low, high):
        lh[:, edge], ll[:, edge] = split(lrx[:, edge])

    def store_l(m, out):
        smooth_o[:, pl.ds(m * LANES, LANES)] = out

    smooth_first((lh, ll), (ah, al), samples, range(blocks + 1))
    l_total = smooth_rest((ah, al), (bh, bl), samples, store_l)
    sums_l[me] = as_row(l_total)
    others(lambda device: remote(sums_l.at[me], sums_l.at[me], 16, device).start())

    pl.when(owner_of(1))(lambda: add_and_return(1))

    def sums_of(ref):
        mean = jnp.sum(ref[...], axis=0) * (1.0 / ndev)

        def earlier(q, acc):
            return acc + jnp.where(q < me, 1.0, 0.0) * (ref[q] - mean)

        return mean, lax.fori_loop(
            0, ndev, earlier, jnp.zeros_like(mean), unroll=ndev <= 32
        )

    wait_bytes(sums_k.at[pl.ds(0, ndev - 1)], rsem.at[17])
    level_o[...] = jnp.zeros_like(level_o)
    many = comps // LANES
    level_o[1 : many + 1, :], level_o[many + 2 : 2 * many + 2, :] = sums_of(sums_k)
    wait_bytes(sums_l.at[pl.ds(0, ndev - 1)], rsem.at[16])
    level_o[0:1, :], level_o[many + 1 : many + 2, :] = sums_of(sums_l)

    for h in range(2):
        whole = pl.ds(h * per_half * rows, per_half * rows)
        rest = pl.ds(h * per_half * rows, (per_half - 1) * rows)
        pl.when(owner_of(h))(lambda: wait_bytes(c2.at[rest], rsem.at[14 + h]))
        pl.when(jnp.logical_not(owner_of(h)))(lambda: wait_bytes(c2.at[whole], rsem.at[14 + h]))
        coef_o[pl.ds(h * group, group), :] = jnp.concatenate(
            [
                c2[pl.ds(h * per_half * rows + c * group, group), :]
                for c in range(comps // LANES)
            ],
            axis=1,
        )

    for h in range(2):
        wait_bytes(recv_l.at[h, pl.ds(0, nb - 1)], ssem.at[h])
    wait_bytes(targets.at[pl.ds(0, nb - 1)], ssem.at[2])
    wait_bytes(valid.at[pl.ds(0, nb - 1)], ssem.at[3])
    for copy in halos + near:
        copy.wait_send()
    for h in range(2):
        whole = pl.ds(h * per_half * rows, per_half * rows)
        rest = pl.ds(h * per_half * rows, (per_half - 1) * rows)

        def drain():
            wait_bytes(part.at[rest], ssem.at[12 + h])
            wait_bytes(gathered.at[pl.ds(0, ndev - 1)], ssem.at[14 + h])

        pl.when(owner_of(h))(drain)
        pl.when(jnp.logical_not(owner_of(h)))(lambda: wait_bytes(part.at[whole], ssem.at[12 + h]))
    wait_bytes(sums_k.at[pl.ds(0, ndev - 1)], ssem.at[17])
    wait_bytes(sums_l.at[pl.ds(0, ndev - 1)], ssem.at[16])


def finish(total_bins, coef_i, smooth_i, skh, skl, level, coef_o, smooth_o, bridge_o):
    samples, bin_dev = smooth_o.shape
    comps = skh.shape[0]
    eye = iota((LANES, LANES), 0) == iota((LANES, LANES), 1)
    coef = coef_i[...]
    coef_o[...] = coef

    def resolve(rows):
        level = jnp.where(eye, jnp.broadcast_to(rows[:1], (LANES, LANES)), 0.0)
        for h in range(comps // LANES):
            level = level - coef[:, h * LANES : (h + 1) * LANES] * rows[h + 1 : h + 2]
        return jnp.sum(level, axis=1, keepdims=True)

    many = comps // LANES + 1
    mean = resolve(level[:many, :]) * (1.0 / bin_dev)
    carry = resolve(level[many : 2 * many, :])
    c_high, c_low = split(coef)
    wide = 2 * LANES
    ones = jnp.where(iota((wide, wide), 0) <= iota((wide, wide), 1), 1.0, 0.0).astype(BF16)
    scale = 1.0 / math.sqrt(total_bins)
    runs = []
    for m in range(bin_dev // wide):
        window = pl.ds(m * wide, wide)
        value = smooth_i[:, window] - (
            mm(c_high, skh[:, window]) + mm(c_low, skh[:, window]) + mm(c_high, skl[:, window])
        )
        smooth_o[:, window] = value
        v_high, v_low = split(value - mean)
        runs.append(mm(v_high, ones) + mm(v_low, ones))
    for m, run in enumerate(runs):
        bridge_o[:, pl.ds(m * wide, wide)] = (run + carry) * scale
        carry = carry + run[:, wide - 1 :]


def in_hbm(x):
    return pltpu.with_memory_space_constraint(x, pltpu.HBM)


def solution(mesh):
    nseg, nb = mesh.shape["seg"], mesh.shape["bin"]
    ndev = nseg * nb

    def per_device(lanes, targets, valid, panel, comp, kern, starts):
        samples = lanes.shape[1]
        comps, bin_dev = comp.shape
        layers, ntaps = kern.shape[:2]
        ext = bin_dev + 2 * LANES
        flat = samples * comps // LANES
        bands = 3 * (bin_dev // LANES) + 2
        vmem, smem = pltpu.VMEM, pltpu.SMEM
        whole = pl.BlockSpec(memory_space=vmem)
        away = pl.BlockSpec(memory_space=pltpu.HBM)
        sds = jax.ShapeDtypeStruct
        coef, smooth, skh, skl, level = pl.pallas_call(
            functools.partial(body, nseg, nb),
            out_shape=(
                sds((samples, comps), F32),
                sds((samples, bin_dev), F32),
                sds((comps, bin_dev), BF16),
                sds((comps, bin_dev), BF16),
                sds((16, LANES), F32),
            ),
            in_specs=[away] * 7,
            out_specs=(whole,) * 5,
            scratch_shapes=[
                smem((nb,) + targets.shape, jnp.int32),
                smem((nb,) + valid.shape, jnp.int32),
                smem(starts.shape, jnp.int32),
                vmem((1, bin_dev), F32),
                vmem((2, nb, samples // 2, LANES), BF16),
                vmem((comps, ext), F32),
                vmem((layers, ntaps, ext), F32),
                vmem((samples, ext), F32),
                vmem((comps, ext), BF16),
                vmem((comps, ext), BF16),
                vmem((samples, ext), BF16),
                vmem((samples, ext), BF16),
                vmem((comps, ext), BF16),
                vmem((comps, ext), BF16),
                vmem((comps, ext), BF16),
                vmem((comps, ext), BF16),
                vmem((bands, 2 * LANES, 2 * LANES), BF16),
                vmem((flat, LANES), F32),
                vmem((ndev, max(8, flat // ndev), LANES), F32),
                vmem((flat, LANES), F32),
                vmem((ndev, 1, LANES), F32),
                vmem((ndev, comps // LANES, LANES), F32),
                vmem((2, LANES, LANES), F32),
                vmem((2, LANES, LANES), F32),
                pltpu.SemaphoreType.DMA((18,)),
                pltpu.SemaphoreType.DMA((18,)),
                pltpu.SemaphoreType.DMA((8,)),
            ],
            compiler_params=pltpu.CompilerParams(
                collective_id=0, has_side_effects=True, vmem_limit_bytes=40 << 20
            ),
        )(*map(in_hbm, (targets, valid, starts, lanes, panel.reshape(1, bin_dev), comp, kern)))
        return pl.pallas_call(
            functools.partial(finish, bin_dev * ndev),
            out_shape=(
                sds((samples, comps), F32),
                sds((samples, bin_dev), F32),
                sds((samples, bin_dev), F32),
            ),
            in_specs=[whole] * 5,
            out_specs=(whole,) * 3,
            compiler_params=pltpu.CompilerParams(vmem_limit_bytes=16 << 20),
        )(coef, smooth, skh, skl, level)

    in_specs = (
        P(("seg", "bin"), None, None),
        P(("seg", "bin")),
        P(("seg", "bin")),
        P(("seg", "bin")),
        P(None, ("seg", "bin")),
        P(None, None, ("seg", "bin")),
        P(),
    )
    out_specs = (P(), P(None, ("seg", "bin")), P(None, ("seg", "bin")))
    return jax.shard_map(
        per_device, mesh=mesh, in_specs=in_specs, out_specs=out_specs, check_vma=False
    )
```

```python
import functools
import math

import jax
import jax.numpy as jnp
from jax import lax
from jax.experimental import pallas as pl
from jax.experimental.pallas import tpu as pltpu
from jax.sharding import PartitionSpec as P

MESH = pl.DeviceIdType.MESH
F32, BF16 = jnp.float32, jnp.bfloat16
LANES = 128


def split(x):
    high = x.astype(BF16)
    return high, (x - high.astype(F32)).astype(BF16)


def mm(a, b, contract=(1, 0)):
    return lax.dot_general(
        a, b, (((contract[0],), (contract[1],)), ((), ())), preferred_element_type=F32
    )


def iota(shape, dim):
    return lax.broadcasted_iota(jnp.int32, shape, dim)


def wait_bytes(ref, sem):
    pltpu.make_async_copy(ref, ref, sem).wait()


def body(
    nseg, nb, targets_h, valid_h, starts_h, lanes_h, panel_h, comp, kern,
    coef_o, smooth_o, skh, skl, level_o,
    targets, valid, starts, panel,
    recv_l, kx, taps, lrx, kh, kl, lh, ll, kah, kal, ah, al, bh, bl,
    weights, masked, part, gathered, c2, sums, spill_out, spill_in, own_w, tout, tin, gout, gin,
    nout, nin, kout, kin, ssem, rsem, lsem,
):
    ndev = nseg * nb
    seg, place = lax.axis_index("seg"), lax.axis_index("bin")
    me = seg * nb + place
    samples, bin_dev = smooth_o.shape
    comps = kx.shape[0]
    blocks = bin_dev // LANES
    total_bins = bin_dev * ndev
    first = me * bin_dev
    ntaps = kern.shape[1]
    half = (ntaps - 1) // 2
    group = samples // 2

    def dev(flat):
        return (lax.div(flat, nb), lax.rem(flat, nb))

    def remote(src, dst, which, device):
        return pltpu.make_async_remote_copy(
            src_ref=src, dst_ref=dst, send_sem=ssem.at[which], recv_sem=rsem.at[which],
            device_id=device, device_id_type=MESH,
        )

    barrier = pltpu.get_barrier_semaphore()

    def each(start, stop, do):
        if stop - start <= 16:
            for hop in range(start, stop):
                do(hop)
        else:
            pl.loop(start, stop)(do)

    def bin_peer(hop):
        return (seg, lax.rem(place + hop, nb))

    def others(do):
        for turn in range(nseg - 1, -1, -1):
            other = lax.rem(seg + turn, nseg)
            each(0 if turn else 1, nb, lambda hop: do((other, lax.rem(place + hop, nb))))

    def swap(out, into, which):
        return [
            remote(out.at[0], into.at[0], which, right),
            remote(out.at[1], into.at[1], which + 1, left),
        ]

    right, left = dev(lax.rem(me + 1, ndev)), dev(lax.rem(me + ndev - 1, ndev))

    others(lambda device: pl.semaphore_signal(
        barrier, inc=1, device_id=device, device_id_type=MESH
    ))

    fetched = [
        pltpu.make_async_copy(src, dst, lsem.at[i])
        for i, (src, dst) in enumerate(
            (
                (starts_h, starts), (kern, taps.at[:, :, pl.ds(LANES, bin_dev)]),
                (panel_h, panel),
                (comp, kx.at[:, pl.ds(LANES, bin_dev)]),
                (targets_h, targets.at[place]), (valid_h, valid.at[place]),
                (lanes_h.at[place, pl.ds(0, group), :], recv_l.at[0, place]),
                (lanes_h.at[place, pl.ds(group, group), :], recv_l.at[1, place]),
            )
        )
    ]
    for copy in fetched:
        copy.start()
    own_s, own_t, own_p, own_k = fetched[:4]

    pl.semaphore_wait(barrier, ndev - 1)

    def mark(hop):
        to = bin_peer(hop)
        remote(targets_h, targets.at[place], 2, to).start()
        remote(valid_h, valid.at[place], 3, to).start()

    each(1, nb, mark)
    def exchange(h):
        def send(hop):
            to = bin_peer(hop)
            remote(
                lanes_h.at[to[1], pl.ds(h * group, group), :], recv_l.at[h, place], h, to
            ).start()

        each(1, nb, send)

    exchange(0)
    low, high = pl.ds(0, LANES), pl.ds(bin_dev + LANES, LANES)
    first_block, last_block = pl.ds(LANES, LANES), pl.ds(bin_dev, LANES)
    tap_halo = swap(tout, tin, 4)
    near = swap(nout, nin, 8)
    k_halo = swap(kout, kin, 6)
    w_halo = swap(gout, gin, 10)
    lower_half = iota((1, LANES), 1) < LANES // 2

    def pack(ref, rows):
        middle = LANES // 2
        return (
            jnp.where(
                lower_half, pltpu.roll(ref[:rows, last_block], middle, 1),
                ref[rows : 2 * rows, last_block],
            ),
            jnp.where(
                lower_half, ref[:rows, first_block],
                pltpu.roll(ref[rows : 2 * rows, first_block], middle, 1),
            ),
        )

    def unpack(ref, h_ref, l_ref, rows):
        for at, edge in enumerate((low, high)):
            turned = pltpu.roll(ref[at], LANES // 2, 1)
            upper, lower = (turned, ref[at]) if at == 0 else (ref[at], turned)
            h_ref[:rows, edge], l_ref[:rows, edge] = split(upper)
            h_ref[rows : 2 * rows, edge], l_ref[rows : 2 * rows, edge] = split(lower)

    own_t.wait()
    wide = 2 * half
    near_end = iota((1, LANES), 1)
    tout[0] = jnp.where(
        near_end >= LANES - wide, taps[0, :, last_block],
        pltpu.roll(taps[1, :, last_block], LANES - wide, 1),
    )
    tout[1] = jnp.where(
        near_end < wide, taps[0, :, first_block], pltpu.roll(taps[1, :, first_block], wide, 1)
    )
    for copy in tap_halo:
        copy.start()
    exchange(1)

    own = pl.ds(LANES, bin_dev)
    for ref in (kah, kal, ah, al, bh, bl):
        ref[:, pl.ds(bin_dev + LANES, LANES)] = jnp.zeros((ref.shape[0], LANES), BF16)
    own_s.wait()

    def band(layer, m, offset, top, base):
        if offset == LANES:
            columns = pl.ds(pl.multiple_of((m + 1) * LANES, LANES), LANES)
            upper = taps[layer, : 2 * half, columns]
            last = taps[layer, 2 * half : ntaps, columns]
        else:
            columns = pl.ds(pl.multiple_of(m * LANES, LANES), 2 * LANES)
            upper = taps[layer, : 2 * half, columns]
            last = taps[layer, 2 * half : ntaps, columns]
        last = jnp.broadcast_to(last, (8, last.shape[1]))
        last = jnp.where(iota(last.shape, 0) == 0, last, 0.0)
        rows = jnp.concatenate([upper, last], axis=0)
        if offset != LANES:
            rows = pltpu.roll(rows, 2 * LANES - offset, 1)[:, :LANES]
        position = first - LANES + offset + m * LANES + iota((8, LANES), 1)
        lower = jnp.full((8, LANES), total_bins, jnp.int32)
        upto = jnp.where(position < total_bins, total_bins, -1)
        count = starts.shape[0]
        for k in range(count):
            lower = jnp.where(starts[k] <= position, starts[k], lower)
        for k in range(count - 1, -1, -1):
            upto = jnp.where(starts[k] > position, starts[k], upto)
        tall = rows.shape[0]
        source = position[:1] + iota((tall, LANES), 0) - half
        inside = (source >= lower[:1]) & (source < upto[:1])
        rows = jnp.where(inside, rows, 0.0)
        masked[base + m] = rows
        lane = iota((1, LANES), 1)
        step = 1
        while step < LANES:
            if step < 8:
                moved = pltpu.roll(rows, step, 0)
                still = rows
            else:
                pad = jnp.zeros((step, LANES), F32)
                moved = jnp.concatenate([pad, rows], axis=0)
                still = jnp.concatenate([rows, pad], axis=0)
            chosen = jnp.broadcast_to((lane & step) != 0, moved.shape)
            rows = jnp.where(chosen, moved, still)
            step *= 2
        rest = 2 * LANES - rows.shape[0] - top
        pieces = [rows, jnp.zeros((rest, LANES), F32)]
        if top:
            pieces = [jnp.zeros((top, LANES), F32)] + pieces
        return split(jnp.concatenate(pieces, axis=0))

    plan = (
        (0, LANES - 2 * half, LANES - 3 * half, 0, blocks + 1),
        (1, LANES - half, 0, blocks + 1, blocks + 1),
        (2, LANES, 0, 2 * blocks + 2, blocks),
    )

    def build(layer, offset, top, base, m):
        w_high, w_low = band(layer, m, offset, top, base)
        weights[base + m, :, :LANES] = w_high
        weights[base + m, :, LANES:] = w_low

    for layer, offset, top, base, many in plan:
        inner = (0, many) if offset == LANES else (1, many - 1)

        @pl.loop(*inner)
        def _(m, layer=layer, offset=offset, top=top, base=base):
            build(layer, offset, top, base, m)

    def smooth_pass(src_high, src_low, m, base):
        window = pl.ds(m * LANES, 2 * LANES)
        both = mm(src_high[:, window], weights[base + m])
        return both[:, :LANES] + both[:, LANES:] + mm(
            src_low[:, window], weights[base + m, :, :LANES]
        )

    def smooth_first(src, mid, rows, which):
        for m in which:
            out = split(smooth_pass(src[0], src[1], m, plan[0][3]))
            for ref, value in zip(mid, out):
                ref[:rows, pl.ds(m * LANES, LANES)] = value

    def smooth_rest(mid, end, rows, store):
        for m in range(blocks + 1):
            out = split(
                smooth_pass(mid[0].at[:rows], mid[1].at[:rows], m, plan[1][3])
            )
            for ref, value in zip(end, out):
                ref[:rows, pl.ds(m * LANES, LANES)] = value
        for m in range(blocks):
            store(m, smooth_pass(end[0].at[:rows], end[1].at[:rows], m, plan[2][3]))

    def adjoint(window, rows, top):
        tall = masked[window] * rows
        turned = pltpu.roll(
            jnp.concatenate([tall, jnp.zeros_like(tall)], axis=1), top, 1, stride=1, stride_axis=0
        )
        return jnp.sum(turned, axis=0, keepdims=True)

    def gradient():
        level = [jnp.ones((1, LANES), F32)] * blocks
        for layer, offset, top, base, many in plan[::-1]:
            parts = [adjoint(base + m, level[m], top) for m in range(many)]
            none = jnp.zeros((1, LANES), F32)
            level = [
                (parts[m][:, :LANES] if m < many else none)
                + (parts[m - 1][:, LANES:] if m else none)
                for m in range(many + 1)
            ]
        return level

    own_k.wait()
    kh[:, own], kl[:, own] = split(kx[:, own])
    smooth_first((kh, kl), (kah, kal), comps, range(1, blocks))
    kout[0], kout[1] = pack(kx, comps // 2)

    def store_k(m, out):
        window = pl.ds(m * LANES, LANES)
        skh[:, window], skl[:, window] = split(out)

    for copy in tap_halo:
        copy.wait_recv()
    taps[0, :, low] = tin[0]
    taps[1, :, low] = pltpu.roll(tin[0], wide, 1)
    taps[0, :, high] = tin[1]
    taps[1, :, high] = pltpu.roll(tin[1], LANES - wide, 1)
    for layer, offset, top, base, many in plan[:2]:
        for m in (0, many - 1):
            build(layer, offset, top, base, m)
    slope = gradient()
    gout[0], gout[1] = slope[blocks + 1], slope[0]
    for copy in w_halo:
        copy.start()
    for m in range(blocks):
        own_w[:, pl.ds(m * LANES, LANES)] = slope[m + 1]

    rows = max(8, part.shape[0] // ndev)
    chunks = part.shape[0] // rows
    stride = ndev // chunks
    mine, side = lax.div(me, 2 * stride), lax.rem(lax.div(me, stride), 2)
    per_half = chunks // 2

    def chunk(h, j):
        return pl.ds(pl.multiple_of((h * per_half + j) * rows, 8), rows)

    def owner_of(h):
        mine_here = side == h
        if stride > 1:
            mine_here = jnp.logical_and(mine_here, lax.rem(me, stride) == 0)
        return mine_here

    own_p.wait()
    for copy in fetched[4:]:
        copy.wait()
    wait_bytes(targets.at[pl.ds(0, nb - 1)], rsem.at[2])
    wait_bytes(valid.at[pl.ds(0, nb - 1)], rsem.at[3])
    lane = iota((group, LANES), 1)

    def reduce_half(h):
        mine_rows = pl.ds(h * group, group)
        wait_bytes(recv_l.at[h, pl.ds(0, nb - 1)], rsem.at[h])
        for b in range(blocks):

            def add(r, acc):
                upto = jnp.where(targets[r, place] == b, valid[r, place], 0)
                return acc + jnp.where(lane < upto, recv_l[h, r].astype(F32), 0.0)

            cover = lax.fori_loop(0, nb, add, jnp.zeros((group, LANES), F32), unroll=nb <= 8)
            value = jnp.log(cover + 1.0) - panel[:, pl.ds(b * LANES, LANES)]
            window = pl.ds((b + 1) * LANES, LANES)
            lrx[mine_rows, window] = value
            lh[mine_rows, window], ll[mine_rows, window] = split(value)
        terms = (
            mm(lh[mine_rows, own], kh[:, own], (1, 1))
            + mm(ll[mine_rows, own], kh[:, own], (1, 1))
            + mm(lh[mine_rows, own], kl[:, own], (1, 1))
        )
        for c in range(comps // LANES):
            part[pl.ds(h * per_half * rows + c * group, group), :] = terms[
                :, c * LANES : (c + 1) * LANES
            ]

        def spread(hop):
            j = lax.rem(mine + hop, per_half)
            flat = (2 * j + h) * stride
            pl.when(flat != me)(remote(
                part.at[chunk(h, j)], gathered.at[me], 12 + h, dev(flat)
            ).start)

        each(0, per_half, spread)

    reduce_half(0)
    reduce_half(1)

    nout[0], nout[1] = pack(lrx, group)
    for copy in near + k_halo:
        copy.start()

    for copy in w_halo:
        copy.wait_recv()
    none = jnp.zeros((1, bin_dev - LANES), F32)
    to_left = jnp.concatenate([gin[0], none], axis=1)
    to_right = jnp.concatenate([none, gin[1]], axis=1)
    weigh = []
    for row in (own_w[...] + to_left + to_right, to_right, to_left):
        weigh += split(row)
    weigh = jnp.concatenate(
        [piece.astype(F32) for piece in weigh] + [jnp.zeros((10, bin_dev), F32)], axis=0
    ).astype(BF16)

    def weighed(h_ref, l_ref):
        upper = mm(weigh, h_ref[:, own], (1, 1))
        lower = mm(weigh, l_ref[:, own], (1, 1))
        return [
            upper[i : i + 1] + upper[i + 1 : i + 2] + lower[i : i + 1] for i in (0, 2, 4)
        ]

    def stacked(l_row, k_row):
        return jnp.concatenate(
            [l_row]
            + [k_row[:, c * LANES : (c + 1) * LANES] for c in range(comps // LANES)]
            + [jnp.zeros((3 - comps // LANES, LANES), F32)],
            axis=0,
        )

    full, over, under = map(stacked, weighed(lh, ll), weighed(kh, kl))
    sums[me] = full
    spill_out[...] = over
    spill = remote(spill_out, spill_in, 17, right)
    spill.start()
    others(lambda device: remote(sums.at[me], sums.at[me], 16, device).start())

    def add_and_return(h):
        gathered[me] = part[chunk(h, mine), :]
        wait_bytes(gathered.at[pl.ds(0, ndev - 1)], rsem.at[12 + h])
        c2[chunk(h, mine), :] = jnp.sum(gathered[...], axis=0)
        others(lambda device: remote(
            c2.at[chunk(h, mine)], c2.at[chunk(h, mine)], 14 + h, device
        ).start())

    pl.when(owner_of(0))(lambda: add_and_return(0))

    for copy in near:
        copy.wait_recv()
    unpack(nin, lh, ll, group)

    def store_l(m, out):
        smooth_o[:, pl.ds(m * LANES, LANES)] = out

    smooth_first((lh, ll), (ah, al), samples, range(blocks + 1))
    smooth_rest((ah, al), (bh, bl), samples, store_l)

    pl.when(owner_of(1))(lambda: add_and_return(1))

    for copy in k_halo:
        copy.wait_recv()
    unpack(kin, kh, kl, comps // 2)
    smooth_first((kh, kl), (kah, kal), comps, (0, blocks))
    smooth_rest((kah, kal), (bh, bl), comps, store_k)

    wait_bytes(sums.at[pl.ds(0, ndev - 1)], rsem.at[16])
    spill.wait_recv()
    mean = jnp.sum(sums[...], axis=0) * (1.0 / ndev)

    def earlier(q, acc):
        return acc + jnp.where(q < me, 1.0, 0.0) * (sums[q] - mean)

    level_o[:4, :] = mean
    level_o[4:, :] = lax.fori_loop(
        0, ndev, earlier, under - spill_in[...], unroll=ndev <= 32
    )

    for h in range(2):
        whole = pl.ds(h * per_half * rows, per_half * rows)
        rest = pl.ds(h * per_half * rows, (per_half - 1) * rows)
        pl.when(owner_of(h))(lambda: wait_bytes(c2.at[rest], rsem.at[14 + h]))
        pl.when(jnp.logical_not(owner_of(h)))(lambda: wait_bytes(c2.at[whole], rsem.at[14 + h]))
        coef_o[pl.ds(h * group, group), :] = jnp.concatenate(
            [
                c2[pl.ds(h * per_half * rows + c * group, group), :]
                for c in range(comps // LANES)
            ],
            axis=1,
        )

    for h in range(2):
        wait_bytes(recv_l.at[h, pl.ds(0, nb - 1)], ssem.at[h])
    wait_bytes(targets.at[pl.ds(0, nb - 1)], ssem.at[2])
    wait_bytes(valid.at[pl.ds(0, nb - 1)], ssem.at[3])
    for copy in tap_halo + w_halo + near + k_halo + [spill]:
        copy.wait_send()
    for h in range(2):
        whole = pl.ds(h * per_half * rows, per_half * rows)
        rest = pl.ds(h * per_half * rows, (per_half - 1) * rows)

        def drain():
            wait_bytes(part.at[rest], ssem.at[12 + h])
            wait_bytes(gathered.at[pl.ds(0, ndev - 1)], ssem.at[14 + h])

        pl.when(owner_of(h))(drain)
        pl.when(jnp.logical_not(owner_of(h)))(lambda: wait_bytes(part.at[whole], ssem.at[12 + h]))
    wait_bytes(sums.at[pl.ds(0, ndev - 1)], ssem.at[16])


def finish(total_bins, coef_i, smooth_i, skh, skl, level, coef_o, smooth_o, bridge_o):
    samples, bin_dev = smooth_o.shape
    comps = skh.shape[0]
    eye = iota((LANES, LANES), 0) == iota((LANES, LANES), 1)
    coef = coef_i[...]
    coef_o[...] = coef

    def resolve(rows):
        level = jnp.where(eye, jnp.broadcast_to(rows[:1], (LANES, LANES)), 0.0)
        for h in range(comps // LANES):
            level = level - coef[:, h * LANES : (h + 1) * LANES] * rows[h + 1 : h + 2]
        return jnp.sum(level, axis=1, keepdims=True)

    mean = resolve(level[:4, :]) * (1.0 / bin_dev)
    carry = resolve(level[4:, :])
    c_high, c_low = split(coef)
    wide = 2 * LANES
    ones = jnp.where(iota((wide, wide), 0) <= iota((wide, wide), 1), 1.0, 0.0).astype(BF16)
    scale = 1.0 / math.sqrt(total_bins)
    runs = []
    for m in range(bin_dev // wide):
        window = pl.ds(m * wide, wide)
        value = smooth_i[:, window] - (
            mm(c_high, skh[:, window]) + mm(c_low, skh[:, window]) + mm(c_high, skl[:, window])
        )
        smooth_o[:, window] = value
        v_high, v_low = split(value - mean)
        runs.append(mm(v_high, ones) + mm(v_low, ones))
    for m, run in enumerate(runs):
        bridge_o[:, pl.ds(m * wide, wide)] = (run + carry) * scale
        carry = carry + run[:, wide - 1 :]


def in_hbm(x):
    return pltpu.with_memory_space_constraint(x, pltpu.HBM)


def solution(mesh):
    nseg, nb = mesh.shape["seg"], mesh.shape["bin"]
    ndev = nseg * nb

    def per_device(lanes, targets, valid, panel, comp, kern, starts):
        samples = lanes.shape[1]
        comps, bin_dev = comp.shape
        layers, ntaps = kern.shape[:2]
        ext = bin_dev + 2 * LANES
        flat = samples * comps // LANES
        bands = 3 * (bin_dev // LANES) + 2
        vmem, smem = pltpu.VMEM, pltpu.SMEM
        whole = pl.BlockSpec(memory_space=vmem)
        away = pl.BlockSpec(memory_space=pltpu.HBM)
        sds = jax.ShapeDtypeStruct
        coef, smooth, skh, skl, level = pl.pallas_call(
            functools.partial(body, nseg, nb),
            out_shape=(
                sds((samples, comps), F32),
                sds((samples, bin_dev), F32),
                sds((comps, bin_dev), BF16),
                sds((comps, bin_dev), BF16),
                sds((8, LANES), F32),
            ),
            in_specs=[away] * 7,
            out_specs=(whole,) * 5,
            scratch_shapes=[
                smem((nb,) + targets.shape, jnp.int32),
                smem((nb,) + valid.shape, jnp.int32),
                smem(starts.shape, jnp.int32),
                vmem((1, bin_dev), F32),
                vmem((2, nb, samples // 2, LANES), BF16),
                vmem((comps, ext), F32),
                vmem((layers, ntaps, ext), F32),
                vmem((samples, ext), F32),
                vmem((comps, ext), BF16),
                vmem((comps, ext), BF16),
                vmem((samples, ext), BF16),
                vmem((samples, ext), BF16),
                vmem((comps, ext), BF16),
                vmem((comps, ext), BF16),
                vmem((samples, ext), BF16),
                vmem((samples, ext), BF16),
                vmem((comps, ext), BF16),
                vmem((comps, ext), BF16),
                vmem((bands, 2 * LANES, 2 * LANES), BF16),
                vmem((bands, ntaps + 7, LANES), F32),
                vmem((flat, LANES), F32),
                vmem((ndev, max(8, flat // ndev), LANES), F32),
                vmem((flat, LANES), F32),
                vmem((ndev, 4, LANES), F32),
                vmem((4, LANES), F32),
                vmem((4, LANES), F32),
                vmem((1, bin_dev), F32),
                vmem((2, ntaps, LANES), F32),
                vmem((2, ntaps, LANES), F32),
                vmem((2, 1, LANES), F32),
                vmem((2, 1, LANES), F32),
                vmem((2, samples // 2, LANES), F32),
                vmem((2, samples // 2, LANES), F32),
                vmem((2, comps // 2, LANES), F32),
                vmem((2, comps // 2, LANES), F32),
                pltpu.SemaphoreType.DMA((18,)),
                pltpu.SemaphoreType.DMA((18,)),
                pltpu.SemaphoreType.DMA((8,)),
            ],
            compiler_params=pltpu.CompilerParams(
                collective_id=0, has_side_effects=True, vmem_limit_bytes=40 << 20
            ),
        )(*map(in_hbm, (targets, valid, starts, lanes, panel.reshape(1, bin_dev), comp, kern)))
        return pl.pallas_call(
            functools.partial(finish, bin_dev * ndev),
            out_shape=(
                sds((samples, comps), F32),
                sds((samples, bin_dev), F32),
                sds((samples, bin_dev), F32),
            ),
            in_specs=[whole] * 5,
            out_specs=(whole,) * 3,
            compiler_params=pltpu.CompilerParams(vmem_limit_bytes=16 << 20),
        )(coef, smooth, skh, skl, level)

    in_specs = (
        P(("seg", "bin"), None, None),
        P(("seg", "bin")),
        P(("seg", "bin")),
        P(("seg", "bin")),
        P(None, ("seg", "bin")),
        P(None, None, ("seg", "bin")),
        P(),
    )
    out_specs = (P(), P(None, ("seg", "bin")), P(None, ("seg", "bin")))
    return jax.shard_map(
        per_device, mesh=mesh, in_specs=in_specs, out_specs=out_specs, check_vma=False
    )
```

```python
import functools
import math

import jax
import jax.numpy as jnp
from jax import lax
from jax.experimental import pallas as pl
from jax.experimental.pallas import tpu as pltpu
from jax.sharding import PartitionSpec as P

MESH = pl.DeviceIdType.MESH
F32, BF16 = jnp.float32, jnp.bfloat16
LANES = 128
GROUPS = 2


def split(x):
    high = x.astype(BF16)
    return high, (x - high.astype(F32)).astype(BF16)


def mm(a, b, contract=(1, 0)):
    return lax.dot_general(
        a, b, (((contract[0],), (contract[1],)), ((), ())), preferred_element_type=F32
    )


def iota(shape, dim):
    return lax.broadcasted_iota(jnp.int32, shape, dim)


def wait_bytes(ref, sem):
    pltpu.make_async_copy(ref, ref, sem).wait()


def body(
    nseg, nb, targets_h, valid_h, starts_h, lanes_h, panel_h, comp, kern,
    coef_o, smooth_o, bridge_o,
    targets, valid, starts, panel,
    recv_l, kx, taps, lrx, kh, kl, kth, ktl, skh, skl, lh, ll, kah, kal, ah, al, bh, bl,
    weights, masked, part, gathered, c2, sums, totals, spill_out, spill_in, own_w, tout, tin, gout, gin,
    nout, nin, kout, kin, ssem, rsem, lsem,
):
    ndev = nseg * nb
    seg, place = lax.axis_index("seg"), lax.axis_index("bin")
    me = seg * nb + place
    samples, bin_dev = smooth_o.shape
    comps = kx.shape[0]
    blocks = bin_dev // LANES
    total_bins = bin_dev * ndev
    first = me * bin_dev
    ntaps = kern.shape[1]
    half = (ntaps - 1) // 2
    group = samples // GROUPS
    pair = samples // 2

    def dev(flat):
        return (lax.div(flat, nb), lax.rem(flat, nb))

    def remote(src, dst, which, device):
        return pltpu.make_async_remote_copy(
            src_ref=src, dst_ref=dst, send_sem=ssem.at[which], recv_sem=rsem.at[which],
            device_id=device, device_id_type=MESH,
        )

    barrier = pltpu.get_barrier_semaphore()

    def each(start, stop, do):
        if stop - start <= 16:
            for hop in range(start, stop):
                do(hop)
        else:
            pl.loop(start, stop)(do)

    def bin_peer(hop):
        return (seg, lax.rem(place + hop, nb))

    def others(do):
        for turn in range(nseg - 1, -1, -1):
            other = lax.rem(seg + turn, nseg)
            each(0 if turn else 1, nb, lambda hop: do((other, lax.rem(place + hop, nb))))

    def swap(out, into, which):
        return [
            remote(out.at[0], into.at[0], which, right),
            remote(out.at[1], into.at[1], which + 1, left),
        ]

    right, left = dev(lax.rem(me + 1, ndev)), dev(lax.rem(me + ndev - 1, ndev))

    def greet(device):
        pl.semaphore_signal(barrier, inc=1, device_id=device, device_id_type=MESH)

    each(1, nb, lambda hop: greet(bin_peer(hop)))
    for hop in range(1, nseg):
        greet((lax.rem(seg + hop, nseg), place))
    greet(right)
    greet(left)

    fetched = [
        pltpu.make_async_copy(src, dst, lsem.at[i])
        for i, (src, dst) in enumerate(
            (
                (starts_h, starts), (kern, taps.at[:, :, pl.ds(LANES, bin_dev)]),
                (panel_h, panel),
                (comp, kx.at[:, pl.ds(LANES, bin_dev)]),
                (targets_h, targets.at[place]), (valid_h, valid.at[place]),
            ) + tuple(
                (lanes_h.at[place, pl.ds(h * group, group), :], recv_l.at[h, place])
                for h in range(GROUPS)
            )
        )
    ]
    for copy in fetched:
        copy.start()
    own_s, own_t, own_p, own_k = fetched[:4]

    pl.semaphore_wait(barrier, nb + nseg)

    def mark(hop):
        to = bin_peer(hop)
        remote(targets_h, targets.at[place], 2, to).start()
        remote(valid_h, valid.at[place], 3, to).start()

    each(1, nb, mark)
    def exchange(h):
        def send(hop):
            to = bin_peer(hop)
            remote(
                lanes_h.at[to[1], pl.ds(h * group, group), :], recv_l.at[h, place], 12 + h, to
            ).start()

        each(1, nb, send)

    exchange(0)
    low, high = pl.ds(0, LANES), pl.ds(bin_dev + LANES, LANES)
    first_block, last_block = pl.ds(LANES, LANES), pl.ds(bin_dev, LANES)
    tap_halo = swap(tout, tin, 4)
    near = swap(nout, nin, 8)
    k_halo = swap(kout, kin, 6)
    w_halo = swap(gout, gin, 10)
    lower_half = iota((1, LANES), 1) < LANES // 2

    def pack(ref, rows):
        middle = LANES // 2
        return (
            jnp.where(
                lower_half, pltpu.roll(ref[:rows, last_block], middle, 1),
                ref[rows : 2 * rows, last_block],
            ),
            jnp.where(
                lower_half, ref[:rows, first_block],
                pltpu.roll(ref[rows : 2 * rows, first_block], middle, 1),
            ),
        )

    def unpack(ref, h_ref, l_ref, rows):
        for at, edge in enumerate((low, high)):
            turned = pltpu.roll(ref[at], LANES // 2, 1)
            upper, lower = (turned, ref[at]) if at == 0 else (ref[at], turned)
            h_ref[:rows, edge], l_ref[:rows, edge] = split(upper)
            h_ref[rows : 2 * rows, edge], l_ref[rows : 2 * rows, edge] = split(lower)

    own_t.wait()
    wide = 2 * half
    near_end = iota((1, LANES), 1)
    tout[0] = jnp.where(
        near_end >= LANES - wide, taps[0, :, last_block],
        pltpu.roll(taps[1, :, last_block], LANES - wide, 1),
    )
    tout[1] = jnp.where(
        near_end < wide, taps[0, :, first_block], pltpu.roll(taps[1, :, first_block], wide, 1)
    )
    for copy in tap_halo:
        copy.start()
    for h in range(1, GROUPS):
        exchange(h)
    own_k.wait()
    kout[0], kout[1] = pack(kx, comps // 2)
    for copy in k_halo:
        copy.start()

    own = pl.ds(LANES, bin_dev)
    for ref in (kah, kal, ah, al, bh, bl):
        ref[:, pl.ds(bin_dev + LANES, LANES)] = jnp.zeros((ref.shape[0], LANES), BF16)
    own_s.wait()

    def band(layer, m, offset, top, base):
        if offset == LANES:
            columns = pl.ds(pl.multiple_of((m + 1) * LANES, LANES), LANES)
            upper = taps[layer, : 2 * half, columns]
            last = taps[layer, 2 * half : ntaps, columns]
        else:
            columns = pl.ds(pl.multiple_of(m * LANES, LANES), 2 * LANES)
            upper = taps[layer, : 2 * half, columns]
            last = taps[layer, 2 * half : ntaps, columns]
        last = jnp.broadcast_to(last, (8, last.shape[1]))
        last = jnp.where(iota(last.shape, 0) == 0, last, 0.0)
        rows = jnp.concatenate([upper, last], axis=0)
        if offset != LANES:
            rows = pltpu.roll(rows, 2 * LANES - offset, 1)[:, :LANES]
        position = first - LANES + offset + m * LANES + iota((8, LANES), 1)
        lower = jnp.full((8, LANES), total_bins, jnp.int32)
        upto = jnp.where(position < total_bins, total_bins, -1)
        count = starts.shape[0]
        for k in range(count):
            lower = jnp.where(starts[k] <= position, starts[k], lower)
        for k in range(count - 1, -1, -1):
            upto = jnp.where(starts[k] > position, starts[k], upto)
        tall = rows.shape[0]
        source = position[:1] + iota((tall, LANES), 0) - half
        inside = (source >= lower[:1]) & (source < upto[:1])
        rows = jnp.where(inside, rows, 0.0)
        masked[base + m] = rows
        lane = iota((1, LANES), 1)
        step = 1
        while step < LANES:
            if step < 8:
                moved = pltpu.roll(rows, step, 0)
                still = rows
            else:
                pad = jnp.zeros((step, LANES), F32)
                moved = jnp.concatenate([pad, rows], axis=0)
                still = jnp.concatenate([rows, pad], axis=0)
            chosen = jnp.broadcast_to((lane & step) != 0, moved.shape)
            rows = jnp.where(chosen, moved, still)
            step *= 2
        rest = 2 * LANES - rows.shape[0] - top
        pieces = [rows, jnp.zeros((rest, LANES), F32)]
        if top:
            pieces = [jnp.zeros((top, LANES), F32)] + pieces
        return split(jnp.concatenate(pieces, axis=0))

    plan = (
        (0, LANES - 2 * half, LANES - 3 * half, 0, blocks + 1),
        (1, LANES - half, 0, blocks + 1, blocks + 1),
        (2, LANES, 0, 2 * blocks + 2, blocks),
    )

    def build(layer, offset, top, base, m):
        w_high, w_low = band(layer, m, offset, top, base)
        weights[base + m, :, :LANES] = w_high
        weights[base + m, :, LANES:] = w_low

    for layer, offset, top, base, many in plan:
        inner = (0, many) if offset == LANES else (1, many - 1)

        @pl.loop(*inner)
        def _(m, layer=layer, offset=offset, top=top, base=base):
            build(layer, offset, top, base, m)

    def smooth_pass(src_high, src_low, m, base):
        window = pl.ds(m * LANES, 2 * LANES)
        both = mm(src_high[:, window], weights[base + m])
        return both[:, :LANES] + both[:, LANES:] + mm(
            src_low[:, window], weights[base + m, :, :LANES]
        )

    def smooth_first(src, mid, rows, which):
        for m in which:
            out = split(smooth_pass(src[0], src[1], m, plan[0][3]))
            for ref, value in zip(mid, out):
                ref[:rows, pl.ds(m * LANES, LANES)] = value

    def smooth_rest(mid, end, rows, store):
        for m in range(blocks + 1):
            out = split(
                smooth_pass(mid[0].at[:rows], mid[1].at[:rows], m, plan[1][3])
            )
            for ref, value in zip(end, out):
                ref[:rows, pl.ds(m * LANES, LANES)] = value
        for m in range(blocks):
            store(m, smooth_pass(end[0].at[:rows], end[1].at[:rows], m, plan[2][3]))

    def adjoint(window, rows, top):
        tall = masked[window] * rows
        turned = pltpu.roll(
            jnp.concatenate([tall, jnp.zeros_like(tall)], axis=1), top, 1, stride=1, stride_axis=0
        )
        return jnp.sum(turned, axis=0, keepdims=True)

    def gradient():
        level = [jnp.ones((1, LANES), F32)] * blocks
        for layer, offset, top, base, many in plan[::-1]:
            parts = [adjoint(base + m, level[m], top) for m in range(many)]
            none = jnp.zeros((1, LANES), F32)
            level = [
                (parts[m][:, :LANES] if m < many else none)
                + (parts[m - 1][:, LANES:] if m else none)
                for m in range(many + 1)
            ]
        return level

    kh[:, own], kl[:, own] = split(kx[:, own])
    kth[...], ktl[...] = split(kx[:, own].T)
    smooth_first((kh, kl), (kah, kal), comps, range(1, blocks))

    def store_k(m, out):
        window = pl.ds(m * LANES, LANES)
        skh[:, window], skl[:, window] = split(out)

    for copy in tap_halo:
        copy.wait_recv()
    taps[0, :, low] = tin[0]
    taps[1, :, low] = pltpu.roll(tin[0], wide, 1)
    taps[0, :, high] = tin[1]
    taps[1, :, high] = pltpu.roll(tin[1], LANES - wide, 1)
    for layer, offset, top, base, many in plan[:2]:
        for m in (0, many - 1):
            build(layer, offset, top, base, m)
    slope = gradient()
    gout[0], gout[1] = slope[blocks + 1], slope[0]
    for copy in w_halo:
        copy.start()
    for m in range(blocks):
        own_w[:, pl.ds(m * LANES, LANES)] = slope[m + 1]

    rows = max(8, part.shape[0] // ndev)
    chunks = part.shape[0] // rows
    stride = ndev // chunks
    mine, side = lax.div(me, GROUPS * stride), lax.rem(lax.div(me, stride), GROUPS)
    per_half = chunks // GROUPS

    def chunk(h, j):
        return pl.ds(pl.multiple_of((h * per_half + j) * rows, 8), rows)

    def owner_of(h):
        mine_here = side == h
        if stride > 1:
            mine_here = jnp.logical_and(mine_here, lax.rem(me, stride) == 0)
        return mine_here

    own_p.wait()
    for copy in fetched[4:]:
        copy.wait()
    wait_bytes(targets.at[pl.ds(0, nb - 1)], rsem.at[2])
    wait_bytes(valid.at[pl.ds(0, nb - 1)], rsem.at[3])
    lane = iota((group, LANES), 1)

    def reduce_half(h):
        mine_rows = pl.ds(h * group, group)
        wait_bytes(recv_l.at[h, pl.ds(0, nb - 1)], rsem.at[12 + h])
        for b in range(blocks):

            def add(r, acc):
                upto = jnp.where(targets[r, place] == b, valid[r, place], 0)
                return acc + jnp.where(lane < upto, recv_l[h, r].astype(F32), 0.0)

            cover = lax.fori_loop(0, nb, add, jnp.zeros((group, LANES), F32), unroll=nb <= 8)
            value = jnp.log(cover + 1.0) - panel[:, pl.ds(b * LANES, LANES)]
            window = pl.ds((b + 1) * LANES, LANES)
            lrx[mine_rows, window] = value
            lh[mine_rows, window], ll[mine_rows, window] = split(value)
        terms = (
            mm(lh[mine_rows, own], kth[...])
            + mm(ll[mine_rows, own], kth[...])
            + mm(lh[mine_rows, own], ktl[...])
        )
        for c in range(comps // LANES):
            part[pl.ds(h * per_half * rows + c * group, group), :] = terms[
                :, c * LANES : (c + 1) * LANES
            ]

        def spread(hop):
            j = lax.rem(mine + hop, per_half)
            flat = (GROUPS * j + h) * stride
            pl.when(flat != me)(remote(
                part.at[chunk(h, j)], gathered.at[me], 12 + GROUPS + h, dev(flat)
            ).start)

        each(0, per_half, spread)

    for h in range(GROUPS):
        reduce_half(h)

    nout[0], nout[1] = pack(lrx, pair)
    for copy in near:
        copy.start()

    for copy in w_halo:
        copy.wait_recv()
    none = jnp.zeros((1, bin_dev - LANES), F32)
    to_left = jnp.concatenate([gin[0], none], axis=1)
    to_right = jnp.concatenate([none, gin[1]], axis=1)
    weigh = []
    for row in (own_w[...] + to_left + to_right, to_right, to_left):
        weigh += split(row)
    weigh = jnp.concatenate(
        [piece.astype(F32) for piece in weigh] + [jnp.zeros((10, bin_dev), F32)], axis=0
    ).astype(BF16)

    def weighed(upper, lower):
        return [
            upper[i : i + 1] + upper[i + 1 : i + 2] + lower[i : i + 1] for i in (0, 2, 4)
        ]

    def stacked(l_row, k_row):
        return jnp.concatenate(
            [l_row]
            + [k_row[:, c * LANES : (c + 1) * LANES] for c in range(comps // LANES)]
            + [jnp.zeros((3 - comps // LANES, LANES), F32)],
            axis=0,
        )

    full, over, under = map(
        stacked,
        weighed(mm(weigh, lh[:, own], (1, 1)), mm(weigh, ll[:, own], (1, 1))),
        weighed(mm(weigh, kth[...]), mm(weigh, ktl[...])),
    )
    sums[place] = full
    spill_out[...] = over
    spill = remote(spill_out, spill_in, 1, right)
    spill.start()
    each(1, nb, lambda hop: remote(sums.at[place], sums.at[place], 0, bin_peer(hop)).start())

    for copy in k_halo:
        copy.wait_recv()
    unpack(kin, kh, kl, comps // 2)
    smooth_first((kh, kl), (kah, kal), comps, (0, blocks))
    smooth_rest((kah, kal), (bh, bl), comps, store_k)

    def add_and_return(h):
        gathered[me] = part[chunk(h, mine), :]
        wait_bytes(gathered.at[pl.ds(0, ndev - 1)], rsem.at[12 + GROUPS + h])
        c2[chunk(h, mine), :] = jnp.sum(gathered[...], axis=0)
        others(lambda device: remote(
            c2.at[chunk(h, mine)], c2.at[chunk(h, mine)], 12 + 2 * GROUPS + h, device
        ).start())

    for h in range(GROUPS):
        pl.when(owner_of(h))(functools.partial(add_and_return, h))

    for copy in near:
        copy.wait_recv()
    unpack(nin, lh, ll, pair)

    def store_l(m, out):
        smooth_o[:, pl.ds(m * LANES, LANES)] = out

    smooth_first((lh, ll), (ah, al), samples, range(blocks + 1))
    smooth_rest((ah, al), (bh, bl), samples, store_l)

    wait_bytes(sums.at[pl.ds(0, nb - 1)], rsem.at[0])
    totals[seg] = jnp.sum(sums[...], axis=0)
    for hop in range(1, nseg):
        remote(
            totals.at[seg], totals.at[seg], 12 + 3 * GROUPS, (lax.rem(seg + hop, nseg), place)
        ).start()

    def ahead_of(count, mine, ref, mean):
        def earlier(q, acc):
            return acc + jnp.where(q < mine, 1.0, 0.0) * (ref[q] - mean)

        return lax.fori_loop(0, count, earlier, jnp.zeros_like(mean), unroll=count <= 8)

    spill.wait_recv()
    wait_bytes(totals.at[pl.ds(0, nseg - 1)], rsem.at[12 + 3 * GROUPS])
    mean = jnp.sum(totals[...], axis=0) * (1.0 / ndev)
    before = under - spill_in[...] + ahead_of(nb, place, sums, mean)
    before = before + ahead_of(nseg, seg, totals, mean * nb)
    mean = mean * (1.0 / bin_dev)
    wide = 2 * LANES
    ones = jnp.where(iota((wide, wide), 0) <= iota((wide, wide), 1), 1.0, 0.0).astype(BF16)
    scale = 1.0 / math.sqrt(total_bins)

    def finish(h):
        mine_rows = pl.ds(h * group, group)
        whole = pl.ds(h * per_half * rows, per_half * rows)
        rest = pl.ds(h * per_half * rows, (per_half - 1) * rows)
        arrived = rsem.at[12 + 2 * GROUPS + h]
        pl.when(owner_of(h))(lambda: wait_bytes(c2.at[rest], arrived))
        pl.when(jnp.logical_not(owner_of(h)))(lambda: wait_bytes(c2.at[whole], arrived))
        coef = jnp.concatenate(
            [
                c2[pl.ds(h * per_half * rows + c * group, group), :]
                for c in range(comps // LANES)
            ],
            axis=1,
        )
        coef_o[mine_rows, :] = coef
        eye = iota((group, LANES), 0) + h * group == iota((group, LANES), 1)

        def resolve(level):
            column = jnp.where(eye, level[:1], 0.0)
            for c in range(comps // LANES):
                column = column - coef[:, c * LANES : (c + 1) * LANES] * level[c + 1 : c + 2]
            return jnp.sum(column, axis=1, keepdims=True)

        middle, carry = resolve(mean), resolve(before)
        c_high, c_low = split(coef)
        both = jnp.concatenate([c_high, c_low], axis=0)
        pieces = []
        for m in range(bin_dev // wide):
            window = pl.ds(m * wide, wide)
            taken = mm(both, skh[:, window])
            value = smooth_o[mine_rows, window] - (
                taken[:group] + taken[group:] + mm(c_high, skl[:, window])
            )
            smooth_o[mine_rows, window] = value
            pieces += split(value - middle)
        run = mm(jnp.concatenate(pieces, axis=0), ones)
        runs = [
            run[2 * m * group : (2 * m + 1) * group] + run[(2 * m + 1) * group : (2 * m + 2) * group]
            for m in range(bin_dev // wide)
        ]
        for m, run in enumerate(runs):
            bridge_o[mine_rows, pl.ds(m * wide, wide)] = (run + carry) * scale
            carry = carry + run[:, wide - 1 :]

    for h in range(GROUPS):
        finish(h)

    for h in range(GROUPS):
        wait_bytes(recv_l.at[h, pl.ds(0, nb - 1)], ssem.at[12 + h])
    wait_bytes(targets.at[pl.ds(0, nb - 1)], ssem.at[2])
    wait_bytes(valid.at[pl.ds(0, nb - 1)], ssem.at[3])
    for copy in tap_halo + w_halo + near + k_halo + [spill]:
        copy.wait_send()
    for h in range(GROUPS):
        whole = pl.ds(h * per_half * rows, per_half * rows)
        rest = pl.ds(h * per_half * rows, (per_half - 1) * rows)

        def drain():
            wait_bytes(part.at[rest], ssem.at[12 + GROUPS + h])
            wait_bytes(gathered.at[pl.ds(0, ndev - 1)], ssem.at[12 + 2 * GROUPS + h])

        pl.when(owner_of(h))(drain)
        pl.when(jnp.logical_not(owner_of(h)))(lambda: wait_bytes(part.at[whole], ssem.at[12 + GROUPS + h]))
    wait_bytes(sums.at[pl.ds(0, nb - 1)], ssem.at[0])
    wait_bytes(totals.at[pl.ds(0, nseg - 1)], ssem.at[12 + 3 * GROUPS])


def store(coef_i, smooth_i, bridge_i, coef_o, smooth_o, bridge_o, sem):
    copies = [
        pltpu.make_async_copy(src, dst, sem.at[i])
        for i, (src, dst) in enumerate(
            ((smooth_i, smooth_o), (bridge_i, bridge_o), (coef_i, coef_o))
        )
    ]
    for copy in copies:
        copy.start()
    for copy in copies:
        copy.wait()


def in_hbm(x):
    return pltpu.with_memory_space_constraint(x, pltpu.HBM)


def solution(mesh):
    nseg, nb = mesh.shape["seg"], mesh.shape["bin"]
    ndev = nseg * nb

    def per_device(lanes, targets, valid, panel, comp, kern, starts):
        samples = lanes.shape[1]
        comps, bin_dev = comp.shape
        layers, ntaps = kern.shape[:2]
        ext = bin_dev + 2 * LANES
        flat = samples * comps // LANES
        bands = 3 * (bin_dev // LANES) + 2
        vmem, smem = pltpu.VMEM, pltpu.SMEM
        whole = pl.BlockSpec(memory_space=vmem)
        away = pl.BlockSpec(memory_space=pltpu.HBM)
        sds = jax.ShapeDtypeStruct
        results = (
            sds((samples, comps), F32),
            sds((samples, bin_dev), F32),
            sds((samples, bin_dev), F32),
        )
        found = pl.pallas_call(
            functools.partial(body, nseg, nb),
            out_shape=results,
            in_specs=[away] * 7,
            out_specs=(whole,) * 3,
            scratch_shapes=[
                smem((nb,) + targets.shape, jnp.int32),
                smem((nb,) + valid.shape, jnp.int32),
                smem(starts.shape, jnp.int32),
                vmem((1, bin_dev), F32),
                vmem((GROUPS, nb, samples // GROUPS, LANES), BF16),
                vmem((comps, ext), F32),
                vmem((layers, ntaps, ext), F32),
                vmem((samples, ext), F32),
                vmem((comps, ext), BF16),
                vmem((comps, ext), BF16),
                vmem((bin_dev, comps), BF16),
                vmem((bin_dev, comps), BF16),
                vmem((comps, bin_dev), BF16),
                vmem((comps, bin_dev), BF16),
                vmem((samples, ext), BF16),
                vmem((samples, ext), BF16),
                vmem((comps, ext), BF16),
                vmem((comps, ext), BF16),
                vmem((samples, ext), BF16),
                vmem((samples, ext), BF16),
                vmem((comps, ext), BF16),
                vmem((comps, ext), BF16),
                vmem((bands, 2 * LANES, 2 * LANES), BF16),
                vmem((bands, ntaps + 7, LANES), F32),
                vmem((flat, LANES), F32),
                vmem((ndev, max(8, flat // ndev), LANES), F32),
                vmem((flat, LANES), F32),
                vmem((nb, 4, LANES), F32),
                vmem((nseg, 4, LANES), F32),
                vmem((4, LANES), F32),
                vmem((4, LANES), F32),
                vmem((1, bin_dev), F32),
                vmem((2, ntaps, LANES), F32),
                vmem((2, ntaps, LANES), F32),
                vmem((2, 1, LANES), F32),
                vmem((2, 1, LANES), F32),
                vmem((2, samples // 2, LANES), F32),
                vmem((2, samples // 2, LANES), F32),
                vmem((2, comps // 2, LANES), F32),
                vmem((2, comps // 2, LANES), F32),
                pltpu.SemaphoreType.DMA((13 + 3 * GROUPS,)),
                pltpu.SemaphoreType.DMA((13 + 3 * GROUPS,)),
                pltpu.SemaphoreType.DMA((6 + GROUPS,)),
            ],
            compiler_params=pltpu.CompilerParams(
                collective_id=0, has_side_effects=True, vmem_limit_bytes=40 << 20
            ),
        )(*map(in_hbm, (targets, valid, starts, lanes, panel.reshape(1, bin_dev), comp, kern)))
        return pl.pallas_call(
            store,
            out_shape=results,
            in_specs=[whole] * 3,
            out_specs=(away,) * 3,
            scratch_shapes=[pltpu.SemaphoreType.DMA((3,))],
            compiler_params=pltpu.CompilerParams(vmem_limit_bytes=16 << 20),
        )(*found)

    in_specs = (
        P(("seg", "bin"), None, None),
        P(("seg", "bin")),
        P(("seg", "bin")),
        P(("seg", "bin")),
        P(None, ("seg", "bin")),
        P(None, None, ("seg", "bin")),
        P(),
    )
    out_specs = (P(), P(None, ("seg", "bin")), P(None, ("seg", "bin")))
    return jax.shard_map(
        per_device, mesh=mesh, in_specs=in_specs, out_specs=out_specs, check_vma=False
    )
```

```python
import functools
import math

import jax
import jax.numpy as jnp
from jax import lax
from jax.experimental import pallas as pl
from jax.experimental.pallas import tpu as pltpu
from jax.sharding import PartitionSpec as P

MESH = pl.DeviceIdType.MESH
F32, BF16 = jnp.float32, jnp.bfloat16
LANES = 128
GROUPS = 2


def split(x):
    high = x.astype(BF16)
    return high, (x - high.astype(F32)).astype(BF16)


def mm(a, b, contract=(1, 0)):
    return lax.dot_general(
        a, b, (((contract[0],), (contract[1],)), ((), ())), preferred_element_type=F32
    )


def iota(shape, dim):
    return lax.broadcasted_iota(jnp.int32, shape, dim)


def wait_bytes(ref, sem):
    pltpu.make_async_copy(ref, ref, sem).wait()


def body(
    nseg, nb, targets_h, valid_h, starts_h, lanes_h, panel_h, comp, kern,
    coef_o, smooth_o, bridge_o,
    targets, valid, starts, panel,
    recv_l, kx, taps, lrx, kh, kl, kth, ktl, skh, skl, lh, ll, kah, kal, ah, al, bh, bl,
    weights, masked, part, gathered, c2, sums, totals, spill_out, spill_in, own_w, tout, tin, gout, gin,
    nout, nin, kout, kin, ssem, rsem, lsem,
):
    ndev = nseg * nb
    seg, place = lax.axis_index("seg"), lax.axis_index("bin")
    me = seg * nb + place
    samples, bin_dev = smooth_o.shape
    comps = kx.shape[0]
    blocks = bin_dev // LANES
    total_bins = bin_dev * ndev
    first = me * bin_dev
    ntaps = kern.shape[1]
    half = (ntaps - 1) // 2
    group = samples // GROUPS
    pair = group // 2

    def dev(flat):
        return (lax.div(flat, nb), lax.rem(flat, nb))

    def remote(src, dst, which, device):
        return pltpu.make_async_remote_copy(
            src_ref=src, dst_ref=dst, send_sem=ssem.at[which], recv_sem=rsem.at[which],
            device_id=device, device_id_type=MESH,
        )

    barrier = pltpu.get_barrier_semaphore()

    def each(start, stop, do):
        if stop - start <= 16:
            for hop in range(start, stop):
                do(hop)
        else:
            pl.loop(start, stop)(do)

    def bin_peer(hop):
        return (seg, lax.rem(place + hop, nb))

    def others(do):
        for turn in range(nseg):
            other = lax.rem(seg + turn, nseg)
            each(0 if turn else 1, nb, lambda hop: do((other, lax.rem(place + hop, nb))))

    def swap(out, into, which):
        return [
            remote(out.at[0], into.at[0], which, right),
            remote(out.at[1], into.at[1], which + 1, left),
        ]

    right, left = dev(lax.rem(me + 1, ndev)), dev(lax.rem(me + ndev - 1, ndev))

    def greet(device):
        pl.semaphore_signal(barrier, inc=1, device_id=device, device_id_type=MESH)

    each(1, nb, lambda hop: greet(bin_peer(hop)))
    for hop in range(1, nseg):
        greet((lax.rem(seg + hop, nseg), place))
    greet(right)
    greet(left)

    fetched = [
        pltpu.make_async_copy(src, dst, lsem.at[i])
        for i, (src, dst) in enumerate(
            (
                (starts_h, starts), (kern, taps.at[:, :, pl.ds(LANES, bin_dev)]),
                (panel_h, panel),
                (comp, kx.at[:, pl.ds(LANES, bin_dev)]),
                (targets_h, targets.at[place]), (valid_h, valid.at[place]),
            ) + tuple(
                (lanes_h.at[place, pl.ds(h * group, group), :], recv_l.at[h, place])
                for h in range(GROUPS)
            )
        )
    ]
    for copy in fetched:
        copy.start()
    own_s, own_t, own_p, own_k = fetched[:4]

    pl.semaphore_wait(barrier, nb + nseg)

    def mark(hop):
        to = bin_peer(hop)
        remote(targets_h, targets.at[place], 2, to).start()
        remote(valid_h, valid.at[place], 3, to).start()

    each(1, nb, mark)
    def exchange(h):
        def send(hop):
            to = bin_peer(hop)
            remote(
                lanes_h.at[to[1], pl.ds(h * group, group), :], recv_l.at[h, place], 12 + h, to
            ).start()

        each(1, nb, send)

    exchange(0)
    low, high = pl.ds(0, LANES), pl.ds(bin_dev + LANES, LANES)
    first_block, last_block = pl.ds(LANES, LANES), pl.ds(bin_dev, LANES)
    tap_halo = swap(tout, tin, 4)
    near = [
        copy
        for h, which in enumerate((8, 13 + 3 * GROUPS))
        for copy in swap(nout.at[h], nin.at[h], which)
    ]
    k_halo = swap(kout, kin, 6)
    w_halo = swap(gout, gin, 10)
    lower_half = iota((1, LANES), 1) < LANES // 2

    def pack(ref, rows):
        middle = LANES // 2
        return (
            jnp.where(
                lower_half, pltpu.roll(ref[:rows, last_block], middle, 1),
                ref[rows : 2 * rows, last_block],
            ),
            jnp.where(
                lower_half, ref[:rows, first_block],
                pltpu.roll(ref[rows : 2 * rows, first_block], middle, 1),
            ),
        )

    def unpack(ref, h_ref, l_ref, rows):
        for at, edge in enumerate((low, high)):
            turned = pltpu.roll(ref[at], LANES // 2, 1)
            upper, lower = (turned, ref[at]) if at == 0 else (ref[at], turned)
            h_ref[:rows, edge], l_ref[:rows, edge] = split(upper)
            h_ref[rows : 2 * rows, edge], l_ref[rows : 2 * rows, edge] = split(lower)

    own_t.wait()
    wide = 2 * half
    near_end = iota((1, LANES), 1)
    tout[0] = jnp.where(
        near_end >= LANES - wide, taps[0, :, last_block],
        pltpu.roll(taps[1, :, last_block], LANES - wide, 1),
    )
    tout[1] = jnp.where(
        near_end < wide, taps[0, :, first_block], pltpu.roll(taps[1, :, first_block], wide, 1)
    )
    for copy in tap_halo:
        copy.start()
    for h in range(1, GROUPS):
        exchange(h)

    own = pl.ds(LANES, bin_dev)
    for ref in (kah, kal, ah, al, bh, bl):
        ref[:, pl.ds(bin_dev + LANES, LANES)] = jnp.zeros((ref.shape[0], LANES), BF16)
    own_s.wait()

    def band(layer, m, offset, top, base):
        if offset == LANES:
            columns = pl.ds(pl.multiple_of((m + 1) * LANES, LANES), LANES)
            upper = taps[layer, : 2 * half, columns]
            last = taps[layer, 2 * half : ntaps, columns]
        else:
            columns = pl.ds(pl.multiple_of(m * LANES, LANES), 2 * LANES)
            upper = taps[layer, : 2 * half, columns]
            last = taps[layer, 2 * half : ntaps, columns]
        last = jnp.broadcast_to(last, (8, last.shape[1]))
        last = jnp.where(iota(last.shape, 0) == 0, last, 0.0)
        rows = jnp.concatenate([upper, last], axis=0)
        if offset != LANES:
            rows = pltpu.roll(rows, 2 * LANES - offset, 1)[:, :LANES]
        position = first - LANES + offset + m * LANES + iota((8, LANES), 1)
        lower = jnp.full((8, LANES), total_bins, jnp.int32)
        upto = jnp.where(position < total_bins, total_bins, -1)
        count = starts.shape[0]
        for k in range(count):
            lower = jnp.where(starts[k] <= position, starts[k], lower)
        for k in range(count - 1, -1, -1):
            upto = jnp.where(starts[k] > position, starts[k], upto)
        tall = rows.shape[0]
        source = position[:1] + iota((tall, LANES), 0) - half
        inside = (source >= lower[:1]) & (source < upto[:1])
        rows = jnp.where(inside, rows, 0.0)
        masked[base + m] = rows
        lane = iota((1, LANES), 1)
        step = 1
        while step < LANES:
            if step < 8:
                moved = pltpu.roll(rows, step, 0)
                still = rows
            else:
                pad = jnp.zeros((step, LANES), F32)
                moved = jnp.concatenate([pad, rows], axis=0)
                still = jnp.concatenate([rows, pad], axis=0)
            chosen = jnp.broadcast_to((lane & step) != 0, moved.shape)
            rows = jnp.where(chosen, moved, still)
            step *= 2
        rest = 2 * LANES - rows.shape[0] - top
        pieces = [rows, jnp.zeros((rest, LANES), F32)]
        if top:
            pieces = [jnp.zeros((top, LANES), F32)] + pieces
        return split(jnp.concatenate(pieces, axis=0))

    plan = (
        (0, LANES - 2 * half, LANES - 3 * half, 0, blocks + 1),
        (1, LANES - half, 0, blocks + 1, blocks + 1),
        (2, LANES, 0, 2 * blocks + 2, blocks),
    )

    def build(layer, offset, top, base, m):
        w_high, w_low = band(layer, m, offset, top, base)
        weights[base + m, :, :LANES] = w_high
        weights[base + m, :, LANES:] = w_low

    for layer, offset, top, base, many in plan:
        inner = (0, many) if offset == LANES else (1, many - 1)

        @pl.loop(*inner)
        def _(m, layer=layer, offset=offset, top=top, base=base):
            build(layer, offset, top, base, m)

    def smooth_pass(src_high, src_low, m, base):
        window = pl.ds(m * LANES, 2 * LANES)
        both = mm(src_high[:, window], weights[base + m])
        return both[:, :LANES] + both[:, LANES:] + mm(
            src_low[:, window], weights[base + m, :, :LANES]
        )

    def smooth_first(src, mid, rows, which):
        for m in which:
            out = split(smooth_pass(src[0], src[1], m, plan[0][3]))
            for ref, value in zip(mid, out):
                ref[:rows, pl.ds(m * LANES, LANES)] = value

    def smooth_rest(mid, end, rows, store):
        for m in range(blocks + 1):
            out = split(
                smooth_pass(mid[0].at[:rows], mid[1].at[:rows], m, plan[1][3])
            )
            for ref, value in zip(end, out):
                ref[:rows, pl.ds(m * LANES, LANES)] = value
        for m in range(blocks):
            store(m, smooth_pass(end[0].at[:rows], end[1].at[:rows], m, plan[2][3]))

    def adjoint(window, rows, top):
        tall = masked[window] * rows
        turned = pltpu.roll(
            jnp.concatenate([tall, jnp.zeros_like(tall)], axis=1), top, 1, stride=1, stride_axis=0
        )
        return jnp.sum(turned, axis=0, keepdims=True)

    def gradient():
        level = [jnp.ones((1, LANES), F32)] * blocks
        for layer, offset, top, base, many in plan[::-1]:
            parts = [adjoint(base + m, level[m], top) for m in range(many)]
            none = jnp.zeros((1, LANES), F32)
            level = [
                (parts[m][:, :LANES] if m < many else none)
                + (parts[m - 1][:, LANES:] if m else none)
                for m in range(many + 1)
            ]
        return level

    own_k.wait()
    kh[:, own], kl[:, own] = split(kx[:, own])
    kth[...], ktl[...] = split(kx[:, own].T)
    smooth_first((kh, kl), (kah, kal), comps, range(1, blocks))
    kout[0], kout[1] = pack(kx, comps // 2)

    def store_k(m, out):
        window = pl.ds(m * LANES, LANES)
        skh[:, window], skl[:, window] = split(out)

    for copy in tap_halo:
        copy.wait_recv()
    taps[0, :, low] = tin[0]
    taps[1, :, low] = pltpu.roll(tin[0], wide, 1)
    taps[0, :, high] = tin[1]
    taps[1, :, high] = pltpu.roll(tin[1], LANES - wide, 1)
    for layer, offset, top, base, many in plan[:2]:
        for m in (0, many - 1):
            build(layer, offset, top, base, m)
    slope = gradient()
    gout[0], gout[1] = slope[blocks + 1], slope[0]
    for copy in w_halo:
        copy.start()
    for m in range(blocks):
        own_w[:, pl.ds(m * LANES, LANES)] = slope[m + 1]

    rows = max(8, part.shape[0] // ndev)
    chunks = part.shape[0] // rows
    stride = ndev // chunks
    mine, side = lax.div(me, GROUPS * stride), lax.rem(lax.div(me, stride), GROUPS)
    per_half = chunks // GROUPS

    def chunk(h, j):
        return pl.ds(pl.multiple_of((h * per_half + j) * rows, 8), rows)

    def owner_of(h):
        mine_here = side == h
        if stride > 1:
            mine_here = jnp.logical_and(mine_here, lax.rem(me, stride) == 0)
        return mine_here

    own_p.wait()
    for copy in fetched[4:]:
        copy.wait()
    wait_bytes(targets.at[pl.ds(0, nb - 1)], rsem.at[2])
    wait_bytes(valid.at[pl.ds(0, nb - 1)], rsem.at[3])
    lane = iota((group, LANES), 1)

    def reduce_half(h):
        mine_rows = pl.ds(h * group, group)
        wait_bytes(recv_l.at[h, pl.ds(0, nb - 1)], rsem.at[12 + h])
        for b in range(blocks):

            def add(r, acc):
                upto = jnp.where(targets[r, place] == b, valid[r, place], 0)
                return acc + jnp.where(lane < upto, recv_l[h, r].astype(F32), 0.0)

            cover = lax.fori_loop(0, nb, add, jnp.zeros((group, LANES), F32), unroll=nb <= 8)
            value = jnp.log(cover + 1.0) - panel[:, pl.ds(b * LANES, LANES)]
            window = pl.ds((b + 1) * LANES, LANES)
            lrx[mine_rows, window] = value
            lh[mine_rows, window], ll[mine_rows, window] = split(value)
        nout[h, 0], nout[h, 1] = pack(lrx.at[mine_rows, :], pair)
        for copy in near[2 * h : 2 * h + 2]:
            copy.start()
        terms = (
            mm(lh[mine_rows, own], kth[...])
            + mm(ll[mine_rows, own], kth[...])
            + mm(lh[mine_rows, own], ktl[...])
        )
        for c in range(comps // LANES):
            part[pl.ds(h * per_half * rows + c * group, group), :] = terms[
                :, c * LANES : (c + 1) * LANES
            ]

        def spread(hop):
            j = lax.rem(mine + hop, per_half)
            flat = (GROUPS * j + h) * stride
            pl.when(flat != me)(remote(
                part.at[chunk(h, j)], gathered.at[me], 12 + GROUPS + h, dev(flat)
            ).start)

        each(0, per_half, spread)

    for h in range(GROUPS):
        reduce_half(h)


    for copy in w_halo:
        copy.wait_recv()
    none = jnp.zeros((1, bin_dev - LANES), F32)
    to_left = jnp.concatenate([gin[0], none], axis=1)
    to_right = jnp.concatenate([none, gin[1]], axis=1)
    weigh = []
    for row in (own_w[...] + to_left + to_right, to_right, to_left):
        weigh += split(row)
    weigh = jnp.concatenate(
        [piece.astype(F32) for piece in weigh] + [jnp.zeros((10, bin_dev), F32)], axis=0
    ).astype(BF16)

    def weighed(upper, lower):
        return [
            upper[i : i + 1] + upper[i + 1 : i + 2] + lower[i : i + 1] for i in (0, 2, 4)
        ]

    def stacked(l_row, k_row):
        return jnp.concatenate(
            [l_row]
            + [k_row[:, c * LANES : (c + 1) * LANES] for c in range(comps // LANES)]
            + [jnp.zeros((3 - comps // LANES, LANES), F32)],
            axis=0,
        )

    full, over, under = map(
        stacked,
        weighed(mm(weigh, lh[:, own], (1, 1)), mm(weigh, ll[:, own], (1, 1))),
        weighed(mm(weigh, kth[...]), mm(weigh, ktl[...])),
    )
    sums[place] = full
    spill_out[...] = over
    spill = remote(spill_out, spill_in, 1, right)
    spill.start()
    each(1, nb, lambda hop: remote(sums.at[place], sums.at[place], 0, bin_peer(hop)).start())

    def add_and_return(h):
        gathered[me] = part[chunk(h, mine), :]
        wait_bytes(gathered.at[pl.ds(0, ndev - 1)], rsem.at[12 + GROUPS + h])
        c2[chunk(h, mine), :] = jnp.sum(gathered[...], axis=0)
        others(lambda device: remote(
            c2.at[chunk(h, mine)], c2.at[chunk(h, mine)], 12 + 2 * GROUPS + h, device
        ).start())

    for copy in k_halo:
        copy.start()
    pl.when(owner_of(0))(functools.partial(add_and_return, 0))
    pl.when(owner_of(1))(functools.partial(add_and_return, 1))

    for copy in near:
        copy.wait_recv()
    for h in range(GROUPS):
        mine_rows = pl.ds(h * group, group)
        unpack(nin.at[h], lh.at[mine_rows, :], ll.at[mine_rows, :], pair)

    def store_l(m, out):
        smooth_o[:, pl.ds(m * LANES, LANES)] = out

    smooth_first((lh, ll), (ah, al), samples, range(blocks + 1))
    smooth_rest((ah, al), (bh, bl), samples, store_l)

    wait_bytes(sums.at[pl.ds(0, nb - 1)], rsem.at[0])
    totals[seg] = jnp.sum(sums[...], axis=0)
    for hop in range(1, nseg):
        remote(
            totals.at[seg], totals.at[seg], 12 + 3 * GROUPS, (lax.rem(seg + hop, nseg), place)
        ).start()

    def ahead_of(count, mine, ref, mean):
        def earlier(q, acc):
            return acc + jnp.where(q < mine, 1.0, 0.0) * (ref[q] - mean)

        return lax.fori_loop(0, count, earlier, jnp.zeros_like(mean), unroll=count <= 8)

    for copy in k_halo:
        copy.wait_recv()
    unpack(kin, kh, kl, comps // 2)
    smooth_first((kh, kl), (kah, kal), comps, (0, blocks))
    smooth_rest((kah, kal), (bh, bl), comps, store_k)

    spill.wait_recv()
    wait_bytes(totals.at[pl.ds(0, nseg - 1)], rsem.at[12 + 3 * GROUPS])
    mean = jnp.sum(totals[...], axis=0) * (1.0 / ndev)
    before = under - spill_in[...] + ahead_of(nb, place, sums, mean)
    before = before + ahead_of(nseg, seg, totals, mean * nb)
    mean = mean * (1.0 / bin_dev)
    wide = 2 * LANES
    ones = jnp.where(iota((wide, wide), 0) <= iota((wide, wide), 1), 1.0, 0.0).astype(BF16)
    scale = 1.0 / math.sqrt(total_bins)

    def finish(h):
        mine_rows = pl.ds(h * group, group)
        whole = pl.ds(h * per_half * rows, per_half * rows)
        rest = pl.ds(h * per_half * rows, (per_half - 1) * rows)
        arrived = rsem.at[12 + 2 * GROUPS + h]
        pl.when(owner_of(h))(lambda: wait_bytes(c2.at[rest], arrived))
        pl.when(jnp.logical_not(owner_of(h)))(lambda: wait_bytes(c2.at[whole], arrived))
        coef = jnp.concatenate(
            [
                c2[pl.ds(h * per_half * rows + c * group, group), :]
                for c in range(comps // LANES)
            ],
            axis=1,
        )
        coef_o[mine_rows, :] = coef
        eye = iota((group, LANES), 0) + h * group == iota((group, LANES), 1)

        def resolve(level):
            column = jnp.where(eye, level[:1], 0.0)
            for c in range(comps // LANES):
                column = column - coef[:, c * LANES : (c + 1) * LANES] * level[c + 1 : c + 2]
            return jnp.sum(column, axis=1, keepdims=True)

        middle, carry = resolve(mean), resolve(before)
        c_high, c_low = split(coef)
        both = jnp.concatenate([c_high, c_low], axis=0)
        pieces = []
        for m in range(bin_dev // wide):
            window = pl.ds(m * wide, wide)
            taken = mm(both, skh[:, window])
            value = smooth_o[mine_rows, window] - (
                taken[:group] + taken[group:] + mm(c_high, skl[:, window])
            )
            smooth_o[mine_rows, window] = value
            pieces += split(value - middle)
        run = mm(jnp.concatenate(pieces, axis=0), ones)
        runs = [
            run[2 * m * group : (2 * m + 1) * group] + run[(2 * m + 1) * group : (2 * m + 2) * group]
            for m in range(bin_dev // wide)
        ]
        for m, run in enumerate(runs):
            bridge_o[mine_rows, pl.ds(m * wide, wide)] = (run + carry) * scale
            carry = carry + run[:, wide - 1 :]

    for h in range(GROUPS):
        finish(h)

    for h in range(GROUPS):
        wait_bytes(recv_l.at[h, pl.ds(0, nb - 1)], ssem.at[12 + h])
    wait_bytes(targets.at[pl.ds(0, nb - 1)], ssem.at[2])
    wait_bytes(valid.at[pl.ds(0, nb - 1)], ssem.at[3])
    for copy in tap_halo + w_halo + near + k_halo + [spill]:
        copy.wait_send()
    for h in range(GROUPS):
        whole = pl.ds(h * per_half * rows, per_half * rows)
        rest = pl.ds(h * per_half * rows, (per_half - 1) * rows)

        def drain():
            wait_bytes(part.at[rest], ssem.at[12 + GROUPS + h])
            wait_bytes(gathered.at[pl.ds(0, ndev - 1)], ssem.at[12 + 2 * GROUPS + h])

        pl.when(owner_of(h))(drain)
        pl.when(jnp.logical_not(owner_of(h)))(lambda: wait_bytes(part.at[whole], ssem.at[12 + GROUPS + h]))
    wait_bytes(sums.at[pl.ds(0, nb - 1)], ssem.at[0])
    wait_bytes(totals.at[pl.ds(0, nseg - 1)], ssem.at[12 + 3 * GROUPS])


def store(coef_i, smooth_i, bridge_i, coef_o, smooth_o, bridge_o, sem):
    copies = [
        pltpu.make_async_copy(src, dst, sem.at[i])
        for i, (src, dst) in enumerate(
            ((smooth_i, smooth_o), (bridge_i, bridge_o), (coef_i, coef_o))
        )
    ]
    for copy in copies:
        copy.start()
    for copy in copies:
        copy.wait()


def in_hbm(x):
    return pltpu.with_memory_space_constraint(x, pltpu.HBM)


def solution(mesh):
    nseg, nb = mesh.shape["seg"], mesh.shape["bin"]
    ndev = nseg * nb

    def per_device(lanes, targets, valid, panel, comp, kern, starts):
        samples = lanes.shape[1]
        comps, bin_dev = comp.shape
        layers, ntaps = kern.shape[:2]
        ext = bin_dev + 2 * LANES
        flat = samples * comps // LANES
        bands = 3 * (bin_dev // LANES) + 2
        vmem, smem = pltpu.VMEM, pltpu.SMEM
        whole = pl.BlockSpec(memory_space=vmem)
        away = pl.BlockSpec(memory_space=pltpu.HBM)
        sds = jax.ShapeDtypeStruct
        results = (
            sds((samples, comps), F32),
            sds((samples, bin_dev), F32),
            sds((samples, bin_dev), F32),
        )
        found = pl.pallas_call(
            functools.partial(body, nseg, nb),
            out_shape=results,
            in_specs=[away] * 7,
            out_specs=(whole,) * 3,
            scratch_shapes=[
                smem((nb,) + targets.shape, jnp.int32),
                smem((nb,) + valid.shape, jnp.int32),
                smem(starts.shape, jnp.int32),
                vmem((1, bin_dev), F32),
                vmem((GROUPS, nb, samples // GROUPS, LANES), BF16),
                vmem((comps, ext), F32),
                vmem((layers, ntaps, ext), F32),
                vmem((samples, ext), F32),
                vmem((comps, ext), BF16),
                vmem((comps, ext), BF16),
                vmem((bin_dev, comps), BF16),
                vmem((bin_dev, comps), BF16),
                vmem((comps, bin_dev), BF16),
                vmem((comps, bin_dev), BF16),
                vmem((samples, ext), BF16),
                vmem((samples, ext), BF16),
                vmem((comps, ext), BF16),
                vmem((comps, ext), BF16),
                vmem((samples, ext), BF16),
                vmem((samples, ext), BF16),
                vmem((comps, ext), BF16),
                vmem((comps, ext), BF16),
                vmem((bands, 2 * LANES, 2 * LANES), BF16),
                vmem((bands, ntaps + 7, LANES), F32),
                vmem((flat, LANES), F32),
                vmem((ndev, max(8, flat // ndev), LANES), F32),
                vmem((flat, LANES), F32),
                vmem((nb, 4, LANES), F32),
                vmem((nseg, 4, LANES), F32),
                vmem((4, LANES), F32),
                vmem((4, LANES), F32),
                vmem((1, bin_dev), F32),
                vmem((2, ntaps, LANES), F32),
                vmem((2, ntaps, LANES), F32),
                vmem((2, 1, LANES), F32),
                vmem((2, 1, LANES), F32),
                vmem((GROUPS, 2, samples // GROUPS // 2, LANES), F32),
                vmem((GROUPS, 2, samples // GROUPS // 2, LANES), F32),
                vmem((2, comps // 2, LANES), F32),
                vmem((2, comps // 2, LANES), F32),
                pltpu.SemaphoreType.DMA((15 + 3 * GROUPS,)),
                pltpu.SemaphoreType.DMA((15 + 3 * GROUPS,)),
                pltpu.SemaphoreType.DMA((6 + GROUPS,)),
            ],
            compiler_params=pltpu.CompilerParams(
                collective_id=0, has_side_effects=True, vmem_limit_bytes=40 << 20
            ),
        )(*map(in_hbm, (targets, valid, starts, lanes, panel.reshape(1, bin_dev), comp, kern)))
        return pl.pallas_call(
            store,
            out_shape=results,
            in_specs=[whole] * 3,
            out_specs=(away,) * 3,
            scratch_shapes=[pltpu.SemaphoreType.DMA((3,))],
            compiler_params=pltpu.CompilerParams(vmem_limit_bytes=16 << 20),
        )(*found)

    in_specs = (
        P(("seg", "bin"), None, None),
        P(("seg", "bin")),
        P(("seg", "bin")),
        P(("seg", "bin")),
        P(None, ("seg", "bin")),
        P(None, None, ("seg", "bin")),
        P(),
    )
    out_specs = (P(), P(None, ("seg", "bin")), P(None, ("seg", "bin")))
    return jax.shard_map(
        per_device, mesh=mesh, in_specs=in_specs, out_specs=out_specs, check_vma=False
    )
```

```python
import functools
import math

import jax
import jax.numpy as jnp
from jax import lax
from jax.experimental import pallas as pl
from jax.experimental.pallas import tpu as pltpu
from jax.sharding import PartitionSpec as P

MESH = pl.DeviceIdType.MESH
F32, BF16 = jnp.float32, jnp.bfloat16
LANES = 128
GROUPS = 2


def split(x):
    high = x.astype(BF16)
    return high, (x - high.astype(F32)).astype(BF16)


def mm(a, b, contract=(1, 0)):
    return lax.dot_general(
        a, b, (((contract[0],), (contract[1],)), ((), ())), preferred_element_type=F32
    )


def iota(shape, dim):
    return lax.broadcasted_iota(jnp.int32, shape, dim)


def wait_bytes(ref, sem):
    pltpu.make_async_copy(ref, ref, sem).wait()


def body(
    nseg, nb, targets_h, valid_h, starts_h, lanes_h, panel_h, comp, kern,
    coef_o, smooth_o, bridge_o, skh, skl, level_o,
    targets, valid, starts, panel,
    recv_l, kx, taps, lrx, kh, kl, kth, ktl, lh, ll, kah, kal, ah, al, bh, bl,
    weights, masked, part, gathered, c2, sums, totals, spill_out, spill_in, own_w, tout, tin, gout, gin,
    nout, nin, kout, kin, ssem, rsem, lsem,
):
    ndev = nseg * nb
    seg, place = lax.axis_index("seg"), lax.axis_index("bin")
    me = seg * nb + place
    samples, bin_dev = smooth_o.shape
    comps = kx.shape[0]
    blocks = bin_dev // LANES
    total_bins = bin_dev * ndev
    first = me * bin_dev
    ntaps = kern.shape[1]
    half = (ntaps - 1) // 2
    group = samples // GROUPS
    pair = group // 2

    def dev(flat):
        return (lax.div(flat, nb), lax.rem(flat, nb))

    def remote(src, dst, which, device):
        return pltpu.make_async_remote_copy(
            src_ref=src, dst_ref=dst, send_sem=ssem.at[which], recv_sem=rsem.at[which],
            device_id=device, device_id_type=MESH,
        )

    barrier = pltpu.get_barrier_semaphore()

    def each(start, stop, do):
        if stop - start <= 16:
            for hop in range(start, stop):
                do(hop)
        else:
            pl.loop(start, stop)(do)

    def bin_peer(hop):
        return (seg, lax.rem(place + hop, nb))

    def others(do):
        for turn in range(nseg):
            other = lax.rem(seg + turn, nseg)
            each(0 if turn else 1, nb, lambda hop: do((other, lax.rem(place + hop, nb))))

    def swap(out, into, which):
        return [
            remote(out.at[0], into.at[0], which, right),
            remote(out.at[1], into.at[1], which + 1, left),
        ]

    right, left = dev(lax.rem(me + 1, ndev)), dev(lax.rem(me + ndev - 1, ndev))

    def greet(device):
        pl.semaphore_signal(barrier, inc=1, device_id=device, device_id_type=MESH)

    each(1, nb, lambda hop: greet(bin_peer(hop)))
    for hop in range(1, nseg):
        greet((lax.rem(seg + hop, nseg), place))
    greet(right)
    greet(left)

    fetched = [
        pltpu.make_async_copy(src, dst, lsem.at[i])
        for i, (src, dst) in enumerate(
            (
                (starts_h, starts), (kern, taps.at[:, :, pl.ds(LANES, bin_dev)]),
                (panel_h, panel),
                (comp, kx.at[:, pl.ds(LANES, bin_dev)]),
                (targets_h, targets.at[place]), (valid_h, valid.at[place]),
            ) + tuple(
                (lanes_h.at[place, pl.ds(h * group, group), :], recv_l.at[h, place])
                for h in range(GROUPS)
            )
        )
    ]
    for copy in fetched:
        copy.start()
    own_s, own_t, own_p, own_k = fetched[:4]

    pl.semaphore_wait(barrier, nb + nseg)

    def mark(hop):
        to = bin_peer(hop)
        remote(targets_h, targets.at[place], 2, to).start()
        remote(valid_h, valid.at[place], 3, to).start()

    each(1, nb, mark)
    def exchange(h):
        def send(hop):
            to = bin_peer(hop)
            remote(
                lanes_h.at[to[1], pl.ds(h * group, group), :], recv_l.at[h, place], 12 + h, to
            ).start()

        each(1, nb, send)

    exchange(0)
    low, high = pl.ds(0, LANES), pl.ds(bin_dev + LANES, LANES)
    first_block, last_block = pl.ds(LANES, LANES), pl.ds(bin_dev, LANES)
    tap_halo = swap(tout, tin, 4)
    near = [
        copy
        for h, which in enumerate((8, 13 + 3 * GROUPS))
        for copy in swap(nout.at[h], nin.at[h], which)
    ]
    k_halo = swap(kout, kin, 6)
    w_halo = swap(gout, gin, 10)
    lower_half = iota((1, LANES), 1) < LANES // 2

    def pack(ref, rows):
        middle = LANES // 2
        return (
            jnp.where(
                lower_half, pltpu.roll(ref[:rows, last_block], middle, 1),
                ref[rows : 2 * rows, last_block],
            ),
            jnp.where(
                lower_half, ref[:rows, first_block],
                pltpu.roll(ref[rows : 2 * rows, first_block], middle, 1),
            ),
        )

    def unpack(ref, h_ref, l_ref, rows):
        for at, edge in enumerate((low, high)):
            turned = pltpu.roll(ref[at], LANES // 2, 1)
            upper, lower = (turned, ref[at]) if at == 0 else (ref[at], turned)
            h_ref[:rows, edge], l_ref[:rows, edge] = split(upper)
            h_ref[rows : 2 * rows, edge], l_ref[rows : 2 * rows, edge] = split(lower)

    own_t.wait()
    wide = 2 * half
    near_end = iota((1, LANES), 1)
    tout[0] = jnp.where(
        near_end >= LANES - wide, taps[0, :, last_block],
        pltpu.roll(taps[1, :, last_block], LANES - wide, 1),
    )
    tout[1] = jnp.where(
        near_end < wide, taps[0, :, first_block], pltpu.roll(taps[1, :, first_block], wide, 1)
    )
    for copy in tap_halo:
        copy.start()
    for h in range(1, GROUPS):
        exchange(h)

    own = pl.ds(LANES, bin_dev)
    for ref in (kah, kal, ah, al, bh, bl):
        ref[:, pl.ds(bin_dev + LANES, LANES)] = jnp.zeros((ref.shape[0], LANES), BF16)
    own_s.wait()

    def band(layer, m, offset, top, base):
        if offset == LANES:
            columns = pl.ds(pl.multiple_of((m + 1) * LANES, LANES), LANES)
            upper = taps[layer, : 2 * half, columns]
            last = taps[layer, 2 * half : ntaps, columns]
        else:
            columns = pl.ds(pl.multiple_of(m * LANES, LANES), 2 * LANES)
            upper = taps[layer, : 2 * half, columns]
            last = taps[layer, 2 * half : ntaps, columns]
        last = jnp.broadcast_to(last, (8, last.shape[1]))
        last = jnp.where(iota(last.shape, 0) == 0, last, 0.0)
        rows = jnp.concatenate([upper, last], axis=0)
        if offset != LANES:
            rows = pltpu.roll(rows, 2 * LANES - offset, 1)[:, :LANES]
        position = first - LANES + offset + m * LANES + iota((8, LANES), 1)
        lower = jnp.full((8, LANES), total_bins, jnp.int32)
        upto = jnp.where(position < total_bins, total_bins, -1)
        count = starts.shape[0]
        for k in range(count):
            lower = jnp.where(starts[k] <= position, starts[k], lower)
        for k in range(count - 1, -1, -1):
            upto = jnp.where(starts[k] > position, starts[k], upto)
        tall = rows.shape[0]
        source = position[:1] + iota((tall, LANES), 0) - half
        inside = (source >= lower[:1]) & (source < upto[:1])
        rows = jnp.where(inside, rows, 0.0)
        masked[base + m] = rows
        lane = iota((1, LANES), 1)
        step = 1
        while step < LANES:
            if step < 8:
                moved = pltpu.roll(rows, step, 0)
                still = rows
            else:
                pad = jnp.zeros((step, LANES), F32)
                moved = jnp.concatenate([pad, rows], axis=0)
                still = jnp.concatenate([rows, pad], axis=0)
            chosen = jnp.broadcast_to((lane & step) != 0, moved.shape)
            rows = jnp.where(chosen, moved, still)
            step *= 2
        rest = 2 * LANES - rows.shape[0] - top
        pieces = [rows, jnp.zeros((rest, LANES), F32)]
        if top:
            pieces = [jnp.zeros((top, LANES), F32)] + pieces
        return split(jnp.concatenate(pieces, axis=0))

    plan = (
        (0, LANES - 2 * half, LANES - 3 * half, 0, blocks + 1),
        (1, LANES - half, 0, blocks + 1, blocks + 1),
        (2, LANES, 0, 2 * blocks + 2, blocks),
    )

    def build(layer, offset, top, base, m):
        w_high, w_low = band(layer, m, offset, top, base)
        weights[base + m, :, :LANES] = w_high
        weights[base + m, :, LANES:] = w_low

    for layer, offset, top, base, many in plan:
        inner = (0, many) if offset == LANES else (1, many - 1)

        @pl.loop(*inner)
        def _(m, layer=layer, offset=offset, top=top, base=base):
            build(layer, offset, top, base, m)

    def smooth_pass(src_high, src_low, m, base):
        window = pl.ds(m * LANES, 2 * LANES)
        both = mm(src_high[:, window], weights[base + m])
        return both[:, :LANES] + both[:, LANES:] + mm(
            src_low[:, window], weights[base + m, :, :LANES]
        )

    def smooth_first(src, mid, rows, which):
        for m in which:
            out = split(smooth_pass(src[0], src[1], m, plan[0][3]))
            for ref, value in zip(mid, out):
                ref[:rows, pl.ds(m * LANES, LANES)] = value

    def smooth_rest(mid, end, rows, store):
        for m in range(blocks + 1):
            out = split(
                smooth_pass(mid[0].at[:rows], mid[1].at[:rows], m, plan[1][3])
            )
            for ref, value in zip(end, out):
                ref[:rows, pl.ds(m * LANES, LANES)] = value
        for m in range(blocks):
            store(m, smooth_pass(end[0].at[:rows], end[1].at[:rows], m, plan[2][3]))

    def adjoint(window, rows, top):
        tall = masked[window] * rows
        turned = pltpu.roll(
            jnp.concatenate([tall, jnp.zeros_like(tall)], axis=1), top, 1, stride=1, stride_axis=0
        )
        return jnp.sum(turned, axis=0, keepdims=True)

    def gradient():
        level = [jnp.ones((1, LANES), F32)] * blocks
        for layer, offset, top, base, many in plan[::-1]:
            parts = [adjoint(base + m, level[m], top) for m in range(many)]
            none = jnp.zeros((1, LANES), F32)
            level = [
                (parts[m][:, :LANES] if m < many else none)
                + (parts[m - 1][:, LANES:] if m else none)
                for m in range(many + 1)
            ]
        return level

    own_k.wait()
    kh[:, own], kl[:, own] = split(kx[:, own])
    kth[...], ktl[...] = split(kx[:, own].T)
    smooth_first((kh, kl), (kah, kal), comps, range(1, blocks))
    kout[0], kout[1] = pack(kx, comps // 2)

    def store_k(m, out):
        window = pl.ds(m * LANES, LANES)
        skh[:, window], skl[:, window] = split(out)

    for copy in tap_halo:
        copy.wait_recv()
    taps[0, :, low] = tin[0]
    taps[1, :, low] = pltpu.roll(tin[0], wide, 1)
    taps[0, :, high] = tin[1]
    taps[1, :, high] = pltpu.roll(tin[1], LANES - wide, 1)
    for layer, offset, top, base, many in plan[:2]:
        for m in (0, many - 1):
            build(layer, offset, top, base, m)
    slope = gradient()
    gout[0], gout[1] = slope[blocks + 1], slope[0]
    for copy in w_halo:
        copy.start()
    for m in range(blocks):
        own_w[:, pl.ds(m * LANES, LANES)] = slope[m + 1]

    rows = max(8, part.shape[0] // ndev)
    chunks = part.shape[0] // rows
    stride = ndev // chunks
    mine, side = lax.div(me, GROUPS * stride), lax.rem(lax.div(me, stride), GROUPS)
    per_half = chunks // GROUPS

    def chunk(h, j):
        return pl.ds(pl.multiple_of((h * per_half + j) * rows, 8), rows)

    def owner_of(h):
        mine_here = side == h
        if stride > 1:
            mine_here = jnp.logical_and(mine_here, lax.rem(me, stride) == 0)
        return mine_here

    own_p.wait()
    for copy in fetched[4:]:
        copy.wait()
    wait_bytes(targets.at[pl.ds(0, nb - 1)], rsem.at[2])
    wait_bytes(valid.at[pl.ds(0, nb - 1)], rsem.at[3])
    lane = iota((group, LANES), 1)

    def reduce_half(h):
        mine_rows = pl.ds(h * group, group)
        wait_bytes(recv_l.at[h, pl.ds(0, nb - 1)], rsem.at[12 + h])
        for b in range(blocks):

            def add(r, acc):
                upto = jnp.where(targets[r, place] == b, valid[r, place], 0)
                return acc + jnp.where(lane < upto, recv_l[h, r].astype(F32), 0.0)

            cover = lax.fori_loop(0, nb, add, jnp.zeros((group, LANES), F32), unroll=nb <= 8)
            value = jnp.log(cover + 1.0) - panel[:, pl.ds(b * LANES, LANES)]
            window = pl.ds((b + 1) * LANES, LANES)
            lrx[mine_rows, window] = value
            lh[mine_rows, window], ll[mine_rows, window] = split(value)
        nout[h, 0], nout[h, 1] = pack(lrx.at[mine_rows, :], pair)
        for copy in near[2 * h : 2 * h + 2]:
            copy.start()
        terms = (
            mm(lh[mine_rows, own], kth[...])
            + mm(ll[mine_rows, own], kth[...])
            + mm(lh[mine_rows, own], ktl[...])
        )
        for c in range(comps // LANES):
            part[pl.ds(h * per_half * rows + c * group, group), :] = terms[
                :, c * LANES : (c + 1) * LANES
            ]

        def spread(hop):
            j = lax.rem(mine + hop, per_half)
            flat = (GROUPS * j + h) * stride
            pl.when(flat != me)(remote(
                part.at[chunk(h, j)], gathered.at[me], 12 + GROUPS + h, dev(flat)
            ).start)

        each(0, per_half, spread)

    for h in range(GROUPS):
        reduce_half(h)


    for copy in w_halo:
        copy.wait_recv()
    none = jnp.zeros((1, bin_dev - LANES), F32)
    to_left = jnp.concatenate([gin[0], none], axis=1)
    to_right = jnp.concatenate([none, gin[1]], axis=1)
    weigh = []
    for row in (own_w[...] + to_left + to_right, to_right, to_left):
        weigh += split(row)
    weigh = jnp.concatenate(
        [piece.astype(F32) for piece in weigh] + [jnp.zeros((10, bin_dev), F32)], axis=0
    ).astype(BF16)

    def weighed(upper, lower):
        return [
            upper[i : i + 1] + upper[i + 1 : i + 2] + lower[i : i + 1] for i in (0, 2, 4)
        ]

    def stacked(l_row, k_row):
        return jnp.concatenate(
            [l_row]
            + [k_row[:, c * LANES : (c + 1) * LANES] for c in range(comps // LANES)]
            + [jnp.zeros((3 - comps // LANES, LANES), F32)],
            axis=0,
        )

    full, over, under = map(
        stacked,
        weighed(mm(weigh, lh[:, own], (1, 1)), mm(weigh, ll[:, own], (1, 1))),
        weighed(mm(weigh, kth[...]), mm(weigh, ktl[...])),
    )
    sums[place] = full
    spill_out[...] = over
    spill = remote(spill_out, spill_in, 1, right)
    spill.start()
    each(1, nb, lambda hop: remote(sums.at[place], sums.at[place], 0, bin_peer(hop)).start())

    def add_and_return(h):
        gathered[me] = part[chunk(h, mine), :]
        wait_bytes(gathered.at[pl.ds(0, ndev - 1)], rsem.at[12 + GROUPS + h])
        c2[chunk(h, mine), :] = jnp.sum(gathered[...], axis=0)
        others(lambda device: remote(
            c2.at[chunk(h, mine)], c2.at[chunk(h, mine)], 12 + 2 * GROUPS + h, device
        ).start())

    for copy in k_halo:
        copy.start()
    pl.when(owner_of(0))(functools.partial(add_and_return, 0))
    pl.when(owner_of(1))(functools.partial(add_and_return, 1))

    for copy in near:
        copy.wait_recv()
    for h in range(GROUPS):
        mine_rows = pl.ds(h * group, group)
        unpack(nin.at[h], lh.at[mine_rows, :], ll.at[mine_rows, :], pair)

    def store_l(m, out):
        smooth_o[:, pl.ds(m * LANES, LANES)] = out

    smooth_first((lh, ll), (ah, al), samples, range(blocks + 1))
    smooth_rest((ah, al), (bh, bl), samples, store_l)

    wait_bytes(sums.at[pl.ds(0, nb - 1)], rsem.at[0])
    totals[seg] = jnp.sum(sums[...], axis=0)
    for hop in range(1, nseg):
        remote(
            totals.at[seg], totals.at[seg], 12 + 3 * GROUPS, (lax.rem(seg + hop, nseg), place)
        ).start()

    def ahead_of(count, mine, ref, mean):
        def earlier(q, acc):
            return acc + jnp.where(q < mine, 1.0, 0.0) * (ref[q] - mean)

        return lax.fori_loop(0, count, earlier, jnp.zeros_like(mean), unroll=count <= 8)

    for copy in k_halo:
        copy.wait_recv()
    unpack(kin, kh, kl, comps // 2)
    smooth_first((kh, kl), (kah, kal), comps, (0, blocks))
    smooth_rest((kah, kal), (bh, bl), comps, store_k)

    spill.wait_recv()
    wait_bytes(totals.at[pl.ds(0, nseg - 1)], rsem.at[12 + 3 * GROUPS])
    mean = jnp.sum(totals[...], axis=0) * (1.0 / ndev)
    before = under - spill_in[...] + ahead_of(nb, place, sums, mean)
    before = before + ahead_of(nseg, seg, totals, mean * nb)
    mean = mean * (1.0 / bin_dev)
    def finish(h):
        mine_rows = pl.ds(h * group, group)
        whole = pl.ds(h * per_half * rows, per_half * rows)
        rest = pl.ds(h * per_half * rows, (per_half - 1) * rows)
        arrived = rsem.at[12 + 2 * GROUPS + h]
        pl.when(owner_of(h))(lambda: wait_bytes(c2.at[rest], arrived))
        pl.when(jnp.logical_not(owner_of(h)))(lambda: wait_bytes(c2.at[whole], arrived))
        coef = jnp.concatenate(
            [
                c2[pl.ds(h * per_half * rows + c * group, group), :]
                for c in range(comps // LANES)
            ],
            axis=1,
        )
        coef_o[mine_rows, :] = coef
        if h < GROUPS - 1:
            combine(
                h, group, total_bins, coef, mean, before, skh, skl,
                smooth_o.at[mine_rows, :], smooth_o.at[mine_rows, :],
                bridge_o.at[mine_rows, :], lambda: None, lambda: None,
            )

    level_o[:4, :], level_o[4:, :] = mean, before
    for h in range(GROUPS):
        finish(h)

    for h in range(GROUPS):
        wait_bytes(recv_l.at[h, pl.ds(0, nb - 1)], ssem.at[12 + h])
    wait_bytes(targets.at[pl.ds(0, nb - 1)], ssem.at[2])
    wait_bytes(valid.at[pl.ds(0, nb - 1)], ssem.at[3])
    for copy in tap_halo + w_halo + near + k_halo + [spill]:
        copy.wait_send()
    for h in range(GROUPS):
        whole = pl.ds(h * per_half * rows, per_half * rows)
        rest = pl.ds(h * per_half * rows, (per_half - 1) * rows)

        def drain():
            wait_bytes(part.at[rest], ssem.at[12 + GROUPS + h])
            wait_bytes(gathered.at[pl.ds(0, ndev - 1)], ssem.at[12 + 2 * GROUPS + h])

        pl.when(owner_of(h))(drain)
        pl.when(jnp.logical_not(owner_of(h)))(lambda: wait_bytes(part.at[whole], ssem.at[12 + GROUPS + h]))
    wait_bytes(sums.at[pl.ds(0, nb - 1)], ssem.at[0])
    wait_bytes(totals.at[pl.ds(0, nseg - 1)], ssem.at[12 + 3 * GROUPS])


def combine(
    h, group, total_bins, coef, mean, before, skh, skl, smooth_i, smooth_o, bridge_o,
    smooth_done, bridge_done,
):
    comps, bin_dev = skh.shape
    wide = 2 * LANES
    count = bin_dev // wide
    ones = jnp.where(iota((wide, wide), 0) <= iota((wide, wide), 1), 1.0, 0.0).astype(BF16)
    scale = 1.0 / math.sqrt(total_bins)
    eye = iota((group, LANES), 0) + h * group == iota((group, LANES), 1)

    def resolve(level):
        column = jnp.where(eye, level[:1], 0.0)
        for c in range(comps // LANES):
            column = column - coef[:, c * LANES : (c + 1) * LANES] * level[c + 1 : c + 2]
        return jnp.sum(column, axis=1, keepdims=True)

    middle, carry = resolve(mean), resolve(before)
    c_high, c_low = split(coef)
    both = jnp.concatenate([c_high, c_low], axis=0)
    pieces = []
    for m in range(count):
        window = pl.ds(m * wide, wide)
        taken = mm(both, skh[:, window])
        value = smooth_i[:, window] - (
            taken[:group] + taken[group:] + mm(c_high, skl[:, window])
        )
        smooth_o[:, window] = value
        pieces += split(value - middle)
    smooth_done()
    run = mm(jnp.concatenate(pieces, axis=0), ones)
    for m in range(count):
        at = 2 * m * group
        part = run[at : at + group] + run[at + group : at + 2 * group]
        bridge_o[:, pl.ds(m * wide, wide)] = (part + carry) * scale
        carry = carry + part[:, wide - 1 :]
    bridge_done()


def close(
    total_bins, coef_i, smooth_i, bridge_i, skh, skl, level,
    coef_o, smooth_o, bridge_o, last_s, last_b, sem,
):
    samples = smooth_i.shape[0]
    group = samples // GROUPS
    ready, last = pl.ds(0, samples - group), pl.ds(samples - group, group)
    copies = [
        pltpu.make_async_copy(smooth_i.at[ready, :], smooth_o.at[ready, :], sem.at[0]),
        pltpu.make_async_copy(bridge_i.at[ready, :], bridge_o.at[ready, :], sem.at[1]),
        pltpu.make_async_copy(coef_i, coef_o, sem.at[2]),
        pltpu.make_async_copy(last_s, smooth_o.at[last, :], sem.at[3]),
        pltpu.make_async_copy(last_b, bridge_o.at[last, :], sem.at[4]),
    ]
    for copy in copies[:3]:
        copy.start()
    combine(
        GROUPS - 1, group, total_bins, coef_i[last, :], level[:4, :], level[4:, :], skh, skl,
        smooth_i.at[last, :], last_s, last_b,
        copies[3].start, copies[4].start,
    )
    for copy in copies:
        copy.wait()


def in_hbm(x):
    return pltpu.with_memory_space_constraint(x, pltpu.HBM)


def solution(mesh):
    nseg, nb = mesh.shape["seg"], mesh.shape["bin"]
    ndev = nseg * nb

    def per_device(lanes, targets, valid, panel, comp, kern, starts):
        samples = lanes.shape[1]
        comps, bin_dev = comp.shape
        layers, ntaps = kern.shape[:2]
        ext = bin_dev + 2 * LANES
        flat = samples * comps // LANES
        bands = 3 * (bin_dev // LANES) + 2
        vmem, smem = pltpu.VMEM, pltpu.SMEM
        whole = pl.BlockSpec(memory_space=vmem)
        away = pl.BlockSpec(memory_space=pltpu.HBM)
        sds = jax.ShapeDtypeStruct
        results = (
            sds((samples, comps), F32),
            sds((samples, bin_dev), F32),
            sds((samples, bin_dev), F32),
        )
        found = pl.pallas_call(
            functools.partial(body, nseg, nb),
            out_shape=results + (
                sds((comps, bin_dev), BF16),
                sds((comps, bin_dev), BF16),
                sds((8, LANES), F32),
            ),
            in_specs=[away] * 7,
            out_specs=(whole,) * 6,
            scratch_shapes=[
                smem((nb,) + targets.shape, jnp.int32),
                smem((nb,) + valid.shape, jnp.int32),
                smem(starts.shape, jnp.int32),
                vmem((1, bin_dev), F32),
                vmem((GROUPS, nb, samples // GROUPS, LANES), BF16),
                vmem((comps, ext), F32),
                vmem((layers, ntaps, ext), F32),
                vmem((samples, ext), F32),
                vmem((comps, ext), BF16),
                vmem((comps, ext), BF16),
                vmem((bin_dev, comps), BF16),
                vmem((bin_dev, comps), BF16),
                vmem((samples, ext), BF16),
                vmem((samples, ext), BF16),
                vmem((comps, ext), BF16),
                vmem((comps, ext), BF16),
                vmem((samples, ext), BF16),
                vmem((samples, ext), BF16),
                vmem((comps, ext), BF16),
                vmem((comps, ext), BF16),
                vmem((bands, 2 * LANES, 2 * LANES), BF16),
                vmem((bands, ntaps + 7, LANES), F32),
                vmem((flat, LANES), F32),
                vmem((ndev, max(8, flat // ndev), LANES), F32),
                vmem((flat, LANES), F32),
                vmem((nb, 4, LANES), F32),
                vmem((nseg, 4, LANES), F32),
                vmem((4, LANES), F32),
                vmem((4, LANES), F32),
                vmem((1, bin_dev), F32),
                vmem((2, ntaps, LANES), F32),
                vmem((2, ntaps, LANES), F32),
                vmem((2, 1, LANES), F32),
                vmem((2, 1, LANES), F32),
                vmem((GROUPS, 2, samples // GROUPS // 2, LANES), F32),
                vmem((GROUPS, 2, samples // GROUPS // 2, LANES), F32),
                vmem((2, comps // 2, LANES), F32),
                vmem((2, comps // 2, LANES), F32),
                pltpu.SemaphoreType.DMA((15 + 3 * GROUPS,)),
                pltpu.SemaphoreType.DMA((15 + 3 * GROUPS,)),
                pltpu.SemaphoreType.DMA((6 + GROUPS,)),
            ],
            compiler_params=pltpu.CompilerParams(
                collective_id=0, has_side_effects=True, vmem_limit_bytes=40 << 20
            ),
        )(*map(in_hbm, (targets, valid, starts, lanes, panel.reshape(1, bin_dev), comp, kern)))
        return pl.pallas_call(
            functools.partial(close, bin_dev * ndev),
            out_shape=results,
            in_specs=[whole] * 6,
            out_specs=(away,) * 3,
            scratch_shapes=[
                vmem((samples // GROUPS, bin_dev), F32),
                vmem((samples // GROUPS, bin_dev), F32),
                pltpu.SemaphoreType.DMA((5,)),
            ],
            compiler_params=pltpu.CompilerParams(vmem_limit_bytes=16 << 20),
        )(*found)

    in_specs = (
        P(("seg", "bin"), None, None),
        P(("seg", "bin")),
        P(("seg", "bin")),
        P(("seg", "bin")),
        P(None, ("seg", "bin")),
        P(None, None, ("seg", "bin")),
        P(),
    )
    out_specs = (P(), P(None, ("seg", "bin")), P(None, ("seg", "bin")))
    return jax.shard_map(
        per_device, mesh=mesh, in_specs=in_specs, out_specs=out_specs, check_vma=False
    )
```

```python
import functools
import math

import jax
import jax.numpy as jnp
from jax import lax
from jax.experimental import pallas as pl
from jax.experimental.pallas import tpu as pltpu
from jax.sharding import PartitionSpec as P

MESH = pl.DeviceIdType.MESH
F32, BF16 = jnp.float32, jnp.bfloat16
LANES = 128
GROUPS = 2


def split(x):
    high = x.astype(BF16)
    return high, (x - high.astype(F32)).astype(BF16)


def mm(a, b, contract=(1, 0)):
    return lax.dot_general(
        a, b, (((contract[0],), (contract[1],)), ((), ())), preferred_element_type=F32
    )


def iota(shape, dim):
    return lax.broadcasted_iota(jnp.int32, shape, dim)


def wait_bytes(ref, sem):
    pltpu.make_async_copy(ref, ref, sem).wait()


def body(
    nseg, nb, targets_h, valid_h, starts_h, lanes_h, panel_h, comp, kern,
    coef_o, smooth_o, bridge_o, skh, skl, level_o,
    targets, valid, starts, panel,
    recv_l, kx, taps, lrx, kh, kl, kth, ktl, lh, ll, kah, kal, ah, al, bh, bl,
    weights, masked, part, gathered, c2, sums, totals, spill_out, spill_in, own_w, tout, tin, gout, gin,
    nout, nin, kout, kin, ssem, rsem, lsem,
):
    ndev = nseg * nb
    seg, place = lax.axis_index("seg"), lax.axis_index("bin")
    me = seg * nb + place
    samples, bin_dev = smooth_o.shape
    comps = kx.shape[0]
    blocks = bin_dev // LANES
    total_bins = bin_dev * ndev
    first = me * bin_dev
    ntaps = kern.shape[1]
    half = (ntaps - 1) // 2
    group = samples // GROUPS
    pair = group // 2

    def dev(flat):
        return (lax.div(flat, nb), lax.rem(flat, nb))

    def remote(src, dst, which, device):
        return pltpu.make_async_remote_copy(
            src_ref=src, dst_ref=dst, send_sem=ssem.at[which], recv_sem=rsem.at[which],
            device_id=device, device_id_type=MESH,
        )

    barrier = pltpu.get_barrier_semaphore()

    def each(start, stop, do):
        if stop - start <= 16:
            for hop in range(start, stop):
                do(hop)
        else:
            pl.loop(start, stop)(do)

    def bin_peer(hop):
        return (seg, lax.rem(place + hop, nb))

    def others(do):
        for turn in range(nseg):
            other = lax.rem(seg + turn, nseg)
            each(0 if turn else 1, nb, lambda hop: do((other, lax.rem(place + hop, nb))))

    def swap(out, into, which):
        return [
            remote(out.at[0], into.at[0], which, right),
            remote(out.at[1], into.at[1], which + 1, left),
        ]

    right, left = dev(lax.rem(me + 1, ndev)), dev(lax.rem(me + ndev - 1, ndev))

    def greet(device):
        pl.semaphore_signal(barrier, inc=1, device_id=device, device_id_type=MESH)

    each(1, nb, lambda hop: greet(bin_peer(hop)))
    for hop in range(1, nseg):
        greet((lax.rem(seg + hop, nseg), place))
    greet(right)
    greet(left)

    fetched = [
        pltpu.make_async_copy(src, dst, lsem.at[i])
        for i, (src, dst) in enumerate(
            (
                (starts_h, starts), (kern, taps.at[:, :, pl.ds(LANES, bin_dev)]),
                (panel_h, panel),
                (comp, kx.at[:, pl.ds(LANES, bin_dev)]),
                (targets_h, targets.at[place]), (valid_h, valid.at[place]),
            ) + tuple(
                (lanes_h.at[place, pl.ds(h * group, group), :], recv_l.at[h, place])
                for h in range(GROUPS)
            )
        )
    ]
    for copy in fetched:
        copy.start()
    own_s, own_t, own_p, own_k = fetched[:4]

    pl.semaphore_wait(barrier, nb + nseg)

    def mark(hop):
        to = bin_peer(hop)
        remote(targets_h, targets.at[place], 2, to).start()
        remote(valid_h, valid.at[place], 3, to).start()

    each(1, nb, mark)
    def exchange(h):
        def send(hop):
            to = bin_peer(hop)
            remote(
                lanes_h.at[to[1], pl.ds(h * group, group), :], recv_l.at[h, place], 12 + h, to
            ).start()

        each(1, nb, send)

    exchange(0)
    low, high = pl.ds(0, LANES), pl.ds(bin_dev + LANES, LANES)
    first_block, last_block = pl.ds(LANES, LANES), pl.ds(bin_dev, LANES)
    tap_halo = swap(tout, tin, 4)
    near = [
        copy
        for h, which in enumerate((8, 13 + 3 * GROUPS))
        for copy in swap(nout.at[h], nin.at[h], which)
    ]
    k_halo = swap(kout, kin, 6)
    w_halo = swap(gout, gin, 10)
    lower_half = iota((1, LANES), 1) < LANES // 2

    def pack(ref, rows):
        middle = LANES // 2
        return (
            jnp.where(
                lower_half, pltpu.roll(ref[:rows, last_block], middle, 1),
                ref[rows : 2 * rows, last_block],
            ),
            jnp.where(
                lower_half, ref[:rows, first_block],
                pltpu.roll(ref[rows : 2 * rows, first_block], middle, 1),
            ),
        )

    def unpack(ref, h_ref, l_ref, rows):
        for at, edge in enumerate((low, high)):
            turned = pltpu.roll(ref[at], LANES // 2, 1)
            upper, lower = (turned, ref[at]) if at == 0 else (ref[at], turned)
            h_ref[:rows, edge], l_ref[:rows, edge] = split(upper)
            h_ref[rows : 2 * rows, edge], l_ref[rows : 2 * rows, edge] = split(lower)

    own_t.wait()
    wide = 2 * half
    near_end = iota((1, LANES), 1)
    tout[0] = jnp.where(
        near_end >= LANES - wide, taps[0, :, last_block],
        pltpu.roll(taps[1, :, last_block], LANES - wide, 1),
    )
    tout[1] = jnp.where(
        near_end < wide, taps[0, :, first_block], pltpu.roll(taps[1, :, first_block], wide, 1)
    )
    for copy in tap_halo:
        copy.start()
    for h in range(1, GROUPS):
        exchange(h)

    own = pl.ds(LANES, bin_dev)
    for ref in (kah, kal, ah, al, bh, bl):
        ref[:, pl.ds(bin_dev + LANES, LANES)] = jnp.zeros((ref.shape[0], LANES), BF16)
    own_s.wait()

    def band(layer, m, offset, top, base):
        if offset == LANES:
            columns = pl.ds(pl.multiple_of((m + 1) * LANES, LANES), LANES)
            upper = taps[layer, : 2 * half, columns]
            last = taps[layer, 2 * half : ntaps, columns]
        else:
            columns = pl.ds(pl.multiple_of(m * LANES, LANES), 2 * LANES)
            upper = taps[layer, : 2 * half, columns]
            last = taps[layer, 2 * half : ntaps, columns]
        last = jnp.broadcast_to(last, (8, last.shape[1]))
        last = jnp.where(iota(last.shape, 0) == 0, last, 0.0)
        rows = jnp.concatenate([upper, last], axis=0)
        if offset != LANES:
            rows = pltpu.roll(rows, 2 * LANES - offset, 1)[:, :LANES]
        position = first - LANES + offset + m * LANES + iota((8, LANES), 1)
        lower = jnp.full((8, LANES), total_bins, jnp.int32)
        upto = jnp.where(position < total_bins, total_bins, -1)
        count = starts.shape[0]
        for k in range(count):
            lower = jnp.where(starts[k] <= position, starts[k], lower)
        for k in range(count - 1, -1, -1):
            upto = jnp.where(starts[k] > position, starts[k], upto)
        tall = rows.shape[0]
        source = position[:1] + iota((tall, LANES), 0) - half
        inside = (source >= lower[:1]) & (source < upto[:1])
        rows = jnp.where(inside, rows, 0.0)
        masked[base + m] = rows
        lane = iota((1, LANES), 1)
        step = 1
        while step < LANES:
            if step < 8:
                moved = pltpu.roll(rows, step, 0)
                still = rows
            else:
                pad = jnp.zeros((step, LANES), F32)
                moved = jnp.concatenate([pad, rows], axis=0)
                still = jnp.concatenate([rows, pad], axis=0)
            chosen = jnp.broadcast_to((lane & step) != 0, moved.shape)
            rows = jnp.where(chosen, moved, still)
            step *= 2
        rest = 2 * LANES - rows.shape[0] - top
        pieces = [rows, jnp.zeros((rest, LANES), F32)]
        if top:
            pieces = [jnp.zeros((top, LANES), F32)] + pieces
        return split(jnp.concatenate(pieces, axis=0))

    plan = (
        (0, LANES - 2 * half, LANES - 3 * half, 0, blocks + 1),
        (1, LANES - half, 0, blocks + 1, blocks + 1),
        (2, LANES, 0, 2 * blocks + 2, blocks),
    )

    def build(layer, offset, top, base, m):
        w_high, w_low = band(layer, m, offset, top, base)
        weights[base + m, :, :LANES] = w_high
        weights[base + m, :, LANES:] = w_low

    for layer, offset, top, base, many in plan:
        inner = (0, many) if offset == LANES else (1, many - 1)

        @pl.loop(*inner)
        def _(m, layer=layer, offset=offset, top=top, base=base):
            build(layer, offset, top, base, m)

    def smooth_pass(src_high, src_low, m, base):
        window = pl.ds(m * LANES, 2 * LANES)
        both = mm(src_high[:, window], weights[base + m])
        return both[:, :LANES] + both[:, LANES:] + mm(
            src_low[:, window], weights[base + m, :, :LANES]
        )

    def smooth_first(src, mid, rows, which):
        for m in which:
            out = split(smooth_pass(src[0], src[1], m, plan[0][3]))
            for ref, value in zip(mid, out):
                ref[:rows, pl.ds(m * LANES, LANES)] = value

    def smooth_rest(mid, end, rows, store):
        for m in range(blocks + 1):
            out = split(
                smooth_pass(mid[0].at[:rows], mid[1].at[:rows], m, plan[1][3])
            )
            for ref, value in zip(end, out):
                ref[:rows, pl.ds(m * LANES, LANES)] = value
        for m in range(blocks):
            store(m, smooth_pass(end[0].at[:rows], end[1].at[:rows], m, plan[2][3]))

    def adjoint(window, rows, top):
        tall = masked[window] * rows
        turned = pltpu.roll(
            jnp.concatenate([tall, jnp.zeros_like(tall)], axis=1), top, 1, stride=1, stride_axis=0
        )
        return jnp.sum(turned, axis=0, keepdims=True)

    def gradient():
        level = [jnp.ones((1, LANES), F32)] * blocks
        for layer, offset, top, base, many in plan[::-1]:
            parts = [adjoint(base + m, level[m], top) for m in range(many)]
            none = jnp.zeros((1, LANES), F32)
            level = [
                (parts[m][:, :LANES] if m < many else none)
                + (parts[m - 1][:, LANES:] if m else none)
                for m in range(many + 1)
            ]
        return level

    own_k.wait()
    kh[:, own], kl[:, own] = split(kx[:, own])
    kth[...], ktl[...] = split(kx[:, own].T)
    smooth_first((kh, kl), (kah, kal), comps, range(1, blocks))
    kout[0], kout[1] = pack(kx, comps // 2)

    def store_k(m, out):
        window = pl.ds(m * LANES, LANES)
        skh[:, window], skl[:, window] = split(out)

    for copy in tap_halo:
        copy.wait_recv()
    taps[0, :, low] = tin[0]
    taps[1, :, low] = pltpu.roll(tin[0], wide, 1)
    taps[0, :, high] = tin[1]
    taps[1, :, high] = pltpu.roll(tin[1], LANES - wide, 1)
    for layer, offset, top, base, many in plan[:2]:
        for m in (0, many - 1):
            build(layer, offset, top, base, m)
    slope = gradient()
    gout[0], gout[1] = slope[blocks + 1], slope[0]
    for copy in w_halo:
        copy.start()
    for m in range(blocks):
        own_w[:, pl.ds(m * LANES, LANES)] = slope[m + 1]

    rows = max(8, part.shape[0] // ndev)
    chunks = part.shape[0] // rows
    stride = ndev // chunks
    mine, side = lax.div(me, GROUPS * stride), lax.rem(lax.div(me, stride), GROUPS)
    per_half = chunks // GROUPS

    def chunk(h, j):
        return pl.ds(pl.multiple_of((h * per_half + j) * rows, 8), rows)

    def owner_of(h):
        mine_here = side == h
        if stride > 1:
            mine_here = jnp.logical_and(mine_here, lax.rem(me, stride) == 0)
        return mine_here

    own_p.wait()
    for copy in fetched[4:]:
        copy.wait()
    wait_bytes(targets.at[pl.ds(0, nb - 1)], rsem.at[2])
    wait_bytes(valid.at[pl.ds(0, nb - 1)], rsem.at[3])
    lane = iota((group, LANES), 1)

    def reduce_half(h):
        mine_rows = pl.ds(h * group, group)
        wait_bytes(recv_l.at[h, pl.ds(0, nb - 1)], rsem.at[12 + h])
        for b in range(blocks):

            def add(r, acc):
                upto = jnp.where(targets[r, place] == b, valid[r, place], 0)
                return acc + jnp.where(lane < upto, recv_l[h, r].astype(F32), 0.0)

            cover = lax.fori_loop(0, nb, add, jnp.zeros((group, LANES), F32), unroll=nb <= 8)
            value = jnp.log(cover + 1.0) - panel[:, pl.ds(b * LANES, LANES)]
            window = pl.ds((b + 1) * LANES, LANES)
            lrx[mine_rows, window] = value
            lh[mine_rows, window], ll[mine_rows, window] = split(value)
        nout[h, 0], nout[h, 1] = pack(lrx.at[mine_rows, :], pair)
        for copy in near[2 * h : 2 * h + 2]:
            copy.start()
        both = mm(
            jnp.concatenate([lh[mine_rows, own], ll[mine_rows, own]], axis=0), kth[...]
        )
        terms = both[:group] + both[group:] + mm(lh[mine_rows, own], ktl[...])
        for c in range(comps // LANES):
            part[pl.ds(h * per_half * rows + c * group, group), :] = terms[
                :, c * LANES : (c + 1) * LANES
            ]

        def spread(hop):
            j = lax.rem(mine + hop, per_half)
            flat = (GROUPS * j + h) * stride
            pl.when(flat != me)(remote(
                part.at[chunk(h, j)], gathered.at[me], 12 + GROUPS + h, dev(flat)
            ).start)

        each(0, per_half, spread)

    for h in range(GROUPS):
        reduce_half(h)


    for copy in w_halo:
        copy.wait_recv()
    none = jnp.zeros((1, bin_dev - LANES), F32)
    to_left = jnp.concatenate([gin[0], none], axis=1)
    to_right = jnp.concatenate([none, gin[1]], axis=1)
    weigh = []
    for row in (own_w[...] + to_left + to_right, to_right, to_left):
        weigh += split(row)
    weigh = jnp.concatenate(
        [piece.astype(F32) for piece in weigh] + [jnp.zeros((10, bin_dev), F32)], axis=0
    ).astype(BF16)

    def weighed(upper, lower):
        return [
            upper[i : i + 1] + upper[i + 1 : i + 2] + lower[i : i + 1] for i in (0, 2, 4)
        ]

    def stacked(l_row, k_row):
        return jnp.concatenate(
            [l_row]
            + [k_row[:, c * LANES : (c + 1) * LANES] for c in range(comps // LANES)]
            + [jnp.zeros((3 - comps // LANES, LANES), F32)],
            axis=0,
        )

    full, over, under = map(
        stacked,
        weighed(mm(weigh, lh[:, own], (1, 1)), mm(weigh, ll[:, own], (1, 1))),
        weighed(mm(weigh, kth[...]), mm(weigh, ktl[...])),
    )
    sums[place] = full
    spill_out[...] = over
    spill = remote(spill_out, spill_in, 1, right)
    spill.start()
    each(1, nb, lambda hop: remote(sums.at[place], sums.at[place], 0, bin_peer(hop)).start())

    def add_and_return(h):
        gathered[me] = part[chunk(h, mine), :]
        wait_bytes(gathered.at[pl.ds(0, ndev - 1)], rsem.at[12 + GROUPS + h])
        c2[chunk(h, mine), :] = jnp.sum(gathered[...], axis=0)
        others(lambda device: remote(
            c2.at[chunk(h, mine)], c2.at[chunk(h, mine)], 12 + 2 * GROUPS + h, device
        ).start())

    for copy in k_halo:
        copy.start()
    pl.when(owner_of(0))(functools.partial(add_and_return, 0))
    pl.when(owner_of(1))(functools.partial(add_and_return, 1))

    for copy in near:
        copy.wait_recv()
    for h in range(GROUPS):
        mine_rows = pl.ds(h * group, group)
        unpack(nin.at[h], lh.at[mine_rows, :], ll.at[mine_rows, :], pair)

    def store_l(m, out):
        smooth_o[:, pl.ds(m * LANES, LANES)] = out

    smooth_first((lh, ll), (ah, al), samples, range(blocks + 1))
    smooth_rest((ah, al), (bh, bl), samples, store_l)

    wait_bytes(sums.at[pl.ds(0, nb - 1)], rsem.at[0])
    totals[seg] = jnp.sum(sums[...], axis=0)
    for hop in range(1, nseg):
        remote(
            totals.at[seg], totals.at[seg], 12 + 3 * GROUPS, (lax.rem(seg + hop, nseg), place)
        ).start()

    def ahead_of(count, mine, ref, mean):
        def earlier(q, acc):
            return acc + jnp.where(q < mine, 1.0, 0.0) * (ref[q] - mean)

        return lax.fori_loop(0, count, earlier, jnp.zeros_like(mean), unroll=count <= 8)

    for copy in k_halo:
        copy.wait_recv()
    unpack(kin, kh, kl, comps // 2)
    smooth_first((kh, kl), (kah, kal), comps, (0, blocks))
    smooth_rest((kah, kal), (bh, bl), comps, store_k)

    spill.wait_recv()
    wait_bytes(totals.at[pl.ds(0, nseg - 1)], rsem.at[12 + 3 * GROUPS])
    mean = jnp.sum(totals[...], axis=0) * (1.0 / ndev)
    before = under - spill_in[...] + ahead_of(nb, place, sums, mean)
    before = before + ahead_of(nseg, seg, totals, mean * nb)
    mean = mean * (1.0 / bin_dev)
    def finish(h):
        mine_rows = pl.ds(h * group, group)
        whole = pl.ds(h * per_half * rows, per_half * rows)
        rest = pl.ds(h * per_half * rows, (per_half - 1) * rows)
        arrived = rsem.at[12 + 2 * GROUPS + h]
        pl.when(owner_of(h))(lambda: wait_bytes(c2.at[rest], arrived))
        pl.when(jnp.logical_not(owner_of(h)))(lambda: wait_bytes(c2.at[whole], arrived))
        coef = jnp.concatenate(
            [
                c2[pl.ds(h * per_half * rows + c * group, group), :]
                for c in range(comps // LANES)
            ],
            axis=1,
        )
        coef_o[mine_rows, :] = coef
        if h < GROUPS - 1:
            combine(
                h, group, total_bins, coef, mean, before, skh, skl,
                smooth_o.at[mine_rows, :], smooth_o.at[mine_rows, :],
                bridge_o.at[mine_rows, :], lambda: None, lambda: None,
            )

    level_o[:4, :], level_o[4:, :] = mean, before
    for h in range(GROUPS):
        finish(h)

    for h in range(GROUPS):
        wait_bytes(recv_l.at[h, pl.ds(0, nb - 1)], ssem.at[12 + h])
    wait_bytes(targets.at[pl.ds(0, nb - 1)], ssem.at[2])
    wait_bytes(valid.at[pl.ds(0, nb - 1)], ssem.at[3])
    for copy in tap_halo + w_halo + near + k_halo + [spill]:
        copy.wait_send()
    for h in range(GROUPS):
        whole = pl.ds(h * per_half * rows, per_half * rows)
        rest = pl.ds(h * per_half * rows, (per_half - 1) * rows)

        def drain():
            wait_bytes(part.at[rest], ssem.at[12 + GROUPS + h])
            wait_bytes(gathered.at[pl.ds(0, ndev - 1)], ssem.at[12 + 2 * GROUPS + h])

        pl.when(owner_of(h))(drain)
        pl.when(jnp.logical_not(owner_of(h)))(lambda: wait_bytes(part.at[whole], ssem.at[12 + GROUPS + h]))
    wait_bytes(sums.at[pl.ds(0, nb - 1)], ssem.at[0])
    wait_bytes(totals.at[pl.ds(0, nseg - 1)], ssem.at[12 + 3 * GROUPS])


def combine(
    h, group, total_bins, coef, mean, before, skh, skl, smooth_i, smooth_o, bridge_o,
    smooth_done, bridge_done,
):
    comps, bin_dev = skh.shape
    wide = 2 * LANES
    count = bin_dev // wide
    ones = jnp.where(iota((wide, wide), 0) <= iota((wide, wide), 1), 1.0, 0.0).astype(BF16)
    scale = 1.0 / math.sqrt(total_bins)
    eye = iota((group, LANES), 0) + h * group == iota((group, LANES), 1)

    def resolve(level):
        column = jnp.where(eye, level[:1], 0.0)
        for c in range(comps // LANES):
            column = column - coef[:, c * LANES : (c + 1) * LANES] * level[c + 1 : c + 2]
        return jnp.sum(column, axis=1, keepdims=True)

    middle, carry = resolve(mean), resolve(before)
    c_high, c_low = split(coef)
    both = jnp.concatenate([c_high, c_low], axis=0)
    pieces = []
    for m in range(count):
        window = pl.ds(m * wide, wide)
        taken = mm(both, skh[:, window])
        value = smooth_i[:, window] - (
            taken[:group] + taken[group:] + mm(c_high, skl[:, window])
        )
        smooth_o[:, window] = value
        pieces += split(value - middle)
    smooth_done()
    run = mm(jnp.concatenate(pieces, axis=0), ones)
    for m in range(count):
        at = 2 * m * group
        part = run[at : at + group] + run[at + group : at + 2 * group]
        bridge_o[:, pl.ds(m * wide, wide)] = (part + carry) * scale
        carry = carry + part[:, wide - 1 :]
    bridge_done()


def close(
    total_bins, coef_i, smooth_i, bridge_i, skh, skl, level,
    coef_o, smooth_o, bridge_o, last_s, last_b, sem,
):
    samples = smooth_i.shape[0]
    group = samples // GROUPS
    ready, last = pl.ds(0, samples - group), pl.ds(samples - group, group)
    copies = [
        pltpu.make_async_copy(smooth_i.at[ready, :], smooth_o.at[ready, :], sem.at[0]),
        pltpu.make_async_copy(bridge_i.at[ready, :], bridge_o.at[ready, :], sem.at[1]),
        pltpu.make_async_copy(coef_i, coef_o, sem.at[2]),
        pltpu.make_async_copy(last_s, smooth_o.at[last, :], sem.at[3]),
        pltpu.make_async_copy(last_b, bridge_o.at[last, :], sem.at[4]),
    ]
    for copy in copies[:3]:
        copy.start()
    combine(
        GROUPS - 1, group, total_bins, coef_i[last, :], level[:4, :], level[4:, :], skh, skl,
        smooth_i.at[last, :], last_s, last_b,
        copies[3].start, copies[4].start,
    )
    for copy in copies:
        copy.wait()


def in_hbm(x):
    return pltpu.with_memory_space_constraint(x, pltpu.HBM)


def solution(mesh):
    nseg, nb = mesh.shape["seg"], mesh.shape["bin"]
    ndev = nseg * nb

    def per_device(lanes, targets, valid, panel, comp, kern, starts):
        samples = lanes.shape[1]
        comps, bin_dev = comp.shape
        layers, ntaps = kern.shape[:2]
        ext = bin_dev + 2 * LANES
        flat = samples * comps // LANES
        bands = 3 * (bin_dev // LANES) + 2
        vmem, smem = pltpu.VMEM, pltpu.SMEM
        whole = pl.BlockSpec(memory_space=vmem)
        away = pl.BlockSpec(memory_space=pltpu.HBM)
        sds = jax.ShapeDtypeStruct
        results = (
            sds((samples, comps), F32),
            sds((samples, bin_dev), F32),
            sds((samples, bin_dev), F32),
        )
        found = pl.pallas_call(
            functools.partial(body, nseg, nb),
            out_shape=results + (
                sds((comps, bin_dev), BF16),
                sds((comps, bin_dev), BF16),
                sds((8, LANES), F32),
            ),
            in_specs=[away] * 7,
            out_specs=(whole,) * 6,
            scratch_shapes=[
                smem((nb,) + targets.shape, jnp.int32),
                smem((nb,) + valid.shape, jnp.int32),
                smem(starts.shape, jnp.int32),
                vmem((1, bin_dev), F32),
                vmem((GROUPS, nb, samples // GROUPS, LANES), BF16),
                vmem((comps, ext), F32),
                vmem((layers, ntaps, ext), F32),
                vmem((samples, ext), F32),
                vmem((comps, ext), BF16),
                vmem((comps, ext), BF16),
                vmem((bin_dev, comps), BF16),
                vmem((bin_dev, comps), BF16),
                vmem((samples, ext), BF16),
                vmem((samples, ext), BF16),
                vmem((comps, ext), BF16),
                vmem((comps, ext), BF16),
                vmem((samples, ext), BF16),
                vmem((samples, ext), BF16),
                vmem((comps, ext), BF16),
                vmem((comps, ext), BF16),
                vmem((bands, 2 * LANES, 2 * LANES), BF16),
                vmem((bands, ntaps + 7, LANES), F32),
                vmem((flat, LANES), F32),
                vmem((ndev, max(8, flat // ndev), LANES), F32),
                vmem((flat, LANES), F32),
                vmem((nb, 4, LANES), F32),
                vmem((nseg, 4, LANES), F32),
                vmem((4, LANES), F32),
                vmem((4, LANES), F32),
                vmem((1, bin_dev), F32),
                vmem((2, ntaps, LANES), F32),
                vmem((2, ntaps, LANES), F32),
                vmem((2, 1, LANES), F32),
                vmem((2, 1, LANES), F32),
                vmem((GROUPS, 2, samples // GROUPS // 2, LANES), F32),
                vmem((GROUPS, 2, samples // GROUPS // 2, LANES), F32),
                vmem((2, comps // 2, LANES), F32),
                vmem((2, comps // 2, LANES), F32),
                pltpu.SemaphoreType.DMA((15 + 3 * GROUPS,)),
                pltpu.SemaphoreType.DMA((15 + 3 * GROUPS,)),
                pltpu.SemaphoreType.DMA((6 + GROUPS,)),
            ],
            compiler_params=pltpu.CompilerParams(
                collective_id=0, has_side_effects=True, vmem_limit_bytes=40 << 20
            ),
        )(*map(in_hbm, (targets, valid, starts, lanes, panel.reshape(1, bin_dev), comp, kern)))
        return pl.pallas_call(
            functools.partial(close, bin_dev * ndev),
            out_shape=results,
            in_specs=[whole] * 6,
            out_specs=(away,) * 3,
            scratch_shapes=[
                vmem((samples // GROUPS, bin_dev), F32),
                vmem((samples // GROUPS, bin_dev), F32),
                pltpu.SemaphoreType.DMA((5,)),
            ],
            compiler_params=pltpu.CompilerParams(vmem_limit_bytes=16 << 20),
        )(*found)

    in_specs = (
        P(("seg", "bin"), None, None),
        P(("seg", "bin")),
        P(("seg", "bin")),
        P(("seg", "bin")),
        P(None, ("seg", "bin")),
        P(None, None, ("seg", "bin")),
        P(),
    )
    out_specs = (P(), P(None, ("seg", "bin")), P(None, ("seg", "bin")))
    return jax.shard_map(
        per_device, mesh=mesh, in_specs=in_specs, out_specs=out_specs, check_vma=False
    )
```

```python
import functools
import math

import jax
import jax.numpy as jnp
from jax import lax
from jax.experimental import pallas as pl
from jax.experimental.pallas import tpu as pltpu
from jax.sharding import PartitionSpec as P

MESH = pl.DeviceIdType.MESH
F32, BF16 = jnp.float32, jnp.bfloat16
LANES = 128
GROUPS = 2


def split(x):
    high = x.astype(BF16)
    return high, (x - high.astype(F32)).astype(BF16)


def mm(a, b, contract=(1, 0)):
    return lax.dot_general(
        a, b, (((contract[0],), (contract[1],)), ((), ())), preferred_element_type=F32
    )


def iota(shape, dim):
    return lax.broadcasted_iota(jnp.int32, shape, dim)


def wait_bytes(ref, sem):
    pltpu.make_async_copy(ref, ref, sem).wait()


def body(
    nseg, nb, targets_h, valid_h, starts_h, lanes_h, panel_h, comp, kern,
    coef_o, smooth_o, bridge_o, skh, skl, level_o,
    targets, valid, starts, panel,
    recv_l, kx, taps, lrx, kh, kl, kth, ktl, lh, ll, kah, kal, ah, al, bh, bl,
    weights, masked, part, gathered, c2, sums, totals, spill_out, spill_in, own_w, tout, tin, gout, gin,
    nout, nin, kout, kin, ssem, rsem, lsem,
):
    ndev = nseg * nb
    seg, place = lax.axis_index("seg"), lax.axis_index("bin")
    me = seg * nb + place
    samples, bin_dev = smooth_o.shape
    comps = kx.shape[0]
    blocks = bin_dev // LANES
    total_bins = bin_dev * ndev
    first = me * bin_dev
    ntaps = kern.shape[1]
    half = (ntaps - 1) // 2
    group = samples // GROUPS
    pair = group // 2

    def dev(flat):
        return (lax.div(flat, nb), lax.rem(flat, nb))

    def remote(src, dst, which, device):
        return pltpu.make_async_remote_copy(
            src_ref=src, dst_ref=dst, send_sem=ssem.at[which], recv_sem=rsem.at[which],
            device_id=device, device_id_type=MESH,
        )

    barrier = pltpu.get_barrier_semaphore()

    def each(start, stop, do):
        if stop - start <= 16:
            for hop in range(start, stop):
                do(hop)
        else:
            pl.loop(start, stop)(do)

    def bin_peer(hop):
        return (seg, lax.rem(place + hop, nb))

    def others(do):
        for turn in range(nseg):
            other = lax.rem(seg + turn, nseg)
            each(0 if turn else 1, nb, lambda hop: do((other, lax.rem(place + hop, nb))))

    def swap(out, into, which):
        return [
            remote(out.at[0], into.at[0], which, right),
            remote(out.at[1], into.at[1], which + 1, left),
        ]

    right, left = dev(lax.rem(me + 1, ndev)), dev(lax.rem(me + ndev - 1, ndev))

    def greet(device):
        pl.semaphore_signal(barrier, inc=1, device_id=device, device_id_type=MESH)

    each(1, nb, lambda hop: greet(bin_peer(hop)))
    for hop in range(1, nseg):
        greet((lax.rem(seg + hop, nseg), place))
    greet(right)
    greet(left)

    fetched = [
        pltpu.make_async_copy(src, dst, lsem.at[i])
        for i, (src, dst) in enumerate(
            (
                (starts_h, starts), (kern, taps.at[:, :, pl.ds(LANES, bin_dev)]),
                (panel_h, panel),
                (comp, kx.at[:, pl.ds(LANES, bin_dev)]),
                (targets_h, targets.at[place]), (valid_h, valid.at[place]),
            ) + tuple(
                (lanes_h.at[place, pl.ds(h * group, group), :], recv_l.at[h, place])
                for h in range(GROUPS)
            )
        )
    ]
    for copy in fetched:
        copy.start()
    own_s, own_t, own_p, own_k = fetched[:4]

    pl.semaphore_wait(barrier, nb + nseg)

    def mark(hop):
        to = bin_peer(hop)
        remote(targets_h, targets.at[place], 2, to).start()
        remote(valid_h, valid.at[place], 3, to).start()

    each(1, nb, mark)
    def exchange(h):
        def send(hop):
            to = bin_peer(hop)
            remote(
                lanes_h.at[to[1], pl.ds(h * group, group), :], recv_l.at[h, place], 12 + h, to
            ).start()

        each(1, nb, send)

    exchange(0)
    low, high = pl.ds(0, LANES), pl.ds(bin_dev + LANES, LANES)
    first_block, last_block = pl.ds(LANES, LANES), pl.ds(bin_dev, LANES)
    tap_halo = swap(tout, tin, 4)
    near = [
        copy
        for h, which in enumerate((8, 13 + 3 * GROUPS))
        for copy in swap(nout.at[h], nin.at[h], which)
    ]
    k_halo = swap(kout, kin, 6)
    w_halo = swap(gout, gin, 10)
    lower_half = iota((1, LANES), 1) < LANES // 2

    def pack(ref, rows):
        middle = LANES // 2
        return (
            jnp.where(
                lower_half, pltpu.roll(ref[:rows, last_block], middle, 1),
                ref[rows : 2 * rows, last_block],
            ),
            jnp.where(
                lower_half, ref[:rows, first_block],
                pltpu.roll(ref[rows : 2 * rows, first_block], middle, 1),
            ),
        )

    def unpack(ref, h_ref, l_ref, rows):
        for at, edge in enumerate((low, high)):
            turned = pltpu.roll(ref[at], LANES // 2, 1)
            upper, lower = (turned, ref[at]) if at == 0 else (ref[at], turned)
            h_ref[:rows, edge], l_ref[:rows, edge] = split(upper)
            h_ref[rows : 2 * rows, edge], l_ref[rows : 2 * rows, edge] = split(lower)

    own_t.wait()
    wide = 2 * half
    near_end = iota((1, LANES), 1)
    tout[0] = jnp.where(
        near_end >= LANES - wide, taps[0, :, last_block],
        pltpu.roll(taps[1, :, last_block], LANES - wide, 1),
    )
    tout[1] = jnp.where(
        near_end < wide, taps[0, :, first_block], pltpu.roll(taps[1, :, first_block], wide, 1)
    )
    for copy in tap_halo:
        copy.start()
    for h in range(1, GROUPS):
        exchange(h)

    own = pl.ds(LANES, bin_dev)
    for ref in (kah, kal, ah, al, bh, bl):
        ref[:, pl.ds(bin_dev + LANES, LANES)] = jnp.zeros((ref.shape[0], LANES), BF16)
    own_s.wait()

    def band(layer, m, offset, top, base):
        if offset == LANES:
            columns = pl.ds(pl.multiple_of((m + 1) * LANES, LANES), LANES)
            upper = taps[layer, : 2 * half, columns]
            last = taps[layer, 2 * half : ntaps, columns]
        else:
            columns = pl.ds(pl.multiple_of(m * LANES, LANES), 2 * LANES)
            upper = taps[layer, : 2 * half, columns]
            last = taps[layer, 2 * half : ntaps, columns]
        last = jnp.broadcast_to(last, (8, last.shape[1]))
        last = jnp.where(iota(last.shape, 0) == 0, last, 0.0)
        rows = jnp.concatenate([upper, last], axis=0)
        if offset != LANES:
            rows = pltpu.roll(rows, 2 * LANES - offset, 1)[:, :LANES]
        position = first - LANES + offset + m * LANES + iota((8, LANES), 1)
        lower = jnp.full((8, LANES), total_bins, jnp.int32)
        upto = jnp.where(position < total_bins, total_bins, -1)
        count = starts.shape[0]
        for k in range(count):
            lower = jnp.where(starts[k] <= position, starts[k], lower)
        for k in range(count - 1, -1, -1):
            upto = jnp.where(starts[k] > position, starts[k], upto)
        tall = rows.shape[0]
        source = position[:1] + iota((tall, LANES), 0) - half
        inside = (source >= lower[:1]) & (source < upto[:1])
        rows = jnp.where(inside, rows, 0.0)
        masked[base + m] = rows
        lane = iota((1, LANES), 1)
        step = 1
        while step < LANES:
            if step < 8:
                moved = pltpu.roll(rows, step, 0)
                still = rows
            else:
                pad = jnp.zeros((step, LANES), F32)
                moved = jnp.concatenate([pad, rows], axis=0)
                still = jnp.concatenate([rows, pad], axis=0)
            chosen = jnp.broadcast_to((lane & step) != 0, moved.shape)
            rows = jnp.where(chosen, moved, still)
            step *= 2
        rest = 2 * LANES - rows.shape[0] - top
        pieces = [rows, jnp.zeros((rest, LANES), F32)]
        if top:
            pieces = [jnp.zeros((top, LANES), F32)] + pieces
        return split(jnp.concatenate(pieces, axis=0))

    plan = (
        (0, LANES - 2 * half, LANES - 3 * half, 0, blocks + 1),
        (1, LANES - half, 0, blocks + 1, blocks + 1),
        (2, LANES, 0, 2 * blocks + 2, blocks),
    )

    def build(layer, offset, top, base, m):
        w_high, w_low = band(layer, m, offset, top, base)
        weights[base + m, :, :LANES] = w_high
        weights[base + m, :, LANES:] = w_low

    for layer, offset, top, base, many in plan:
        inner = (0, many) if offset == LANES else (1, many - 1)

        @pl.loop(*inner)
        def _(m, layer=layer, offset=offset, top=top, base=base):
            build(layer, offset, top, base, m)

    def smooth_pass(src_high, src_low, m, base):
        window = pl.ds(m * LANES, 2 * LANES)
        both = mm(src_high[:, window], weights[base + m])
        return both[:, :LANES] + both[:, LANES:] + mm(
            src_low[:, window], weights[base + m, :, :LANES]
        )

    def smooth_first(src, mid, rows, which):
        for m in which:
            out = split(smooth_pass(src[0], src[1], m, plan[0][3]))
            for ref, value in zip(mid, out):
                ref[:rows, pl.ds(m * LANES, LANES)] = value

    def smooth_rest(mid, end, rows, store):
        for m in range(blocks + 1):
            out = split(
                smooth_pass(mid[0].at[:rows], mid[1].at[:rows], m, plan[1][3])
            )
            for ref, value in zip(end, out):
                ref[:rows, pl.ds(m * LANES, LANES)] = value
        for m in range(blocks):
            store(m, smooth_pass(end[0].at[:rows], end[1].at[:rows], m, plan[2][3]))

    def adjoint(window, rows, top):
        tall = masked[window] * rows
        turned = pltpu.roll(
            jnp.concatenate([tall, jnp.zeros_like(tall)], axis=1), top, 1, stride=1, stride_axis=0
        )
        return jnp.sum(turned, axis=0, keepdims=True)

    def gradient():
        level = [jnp.ones((1, LANES), F32)] * blocks
        for layer, offset, top, base, many in plan[::-1]:
            parts = [adjoint(base + m, level[m], top) for m in range(many)]
            none = jnp.zeros((1, LANES), F32)
            level = [
                (parts[m][:, :LANES] if m < many else none)
                + (parts[m - 1][:, LANES:] if m else none)
                for m in range(many + 1)
            ]
        return level

    own_k.wait()
    kh[:, own], kl[:, own] = split(kx[:, own])
    kth[...], ktl[...] = split(kx[:, own].T)
    smooth_first((kh, kl), (kah, kal), comps, range(1, blocks))
    kout[0], kout[1] = pack(kx, comps // 2)

    def store_k(m, out):
        window = pl.ds(m * LANES, LANES)
        skh[:, window], skl[:, window] = split(out)

    for copy in tap_halo:
        copy.wait_recv()
    taps[0, :, low] = tin[0]
    taps[1, :, low] = pltpu.roll(tin[0], wide, 1)
    taps[0, :, high] = tin[1]
    taps[1, :, high] = pltpu.roll(tin[1], LANES - wide, 1)
    for layer, offset, top, base, many in plan[:2]:
        for m in (0, many - 1):
            build(layer, offset, top, base, m)
    slope = gradient()
    gout[0], gout[1] = slope[blocks + 1], slope[0]
    for copy in w_halo:
        copy.start()
    for m in range(blocks):
        own_w[:, pl.ds(m * LANES, LANES)] = slope[m + 1]

    rows = max(8, part.shape[0] // ndev)
    chunks = part.shape[0] // rows
    stride = ndev // chunks
    mine, side = lax.div(me, GROUPS * stride), lax.rem(lax.div(me, stride), GROUPS)
    per_half = chunks // GROUPS

    def chunk(h, j):
        return pl.ds(pl.multiple_of((h * per_half + j) * rows, 8), rows)

    def owner_of(h):
        mine_here = side == h
        if stride > 1:
            mine_here = jnp.logical_and(mine_here, lax.rem(me, stride) == 0)
        return mine_here

    own_p.wait()
    for copy in fetched[4:]:
        copy.wait()
    wait_bytes(targets.at[pl.ds(0, nb - 1)], rsem.at[2])
    wait_bytes(valid.at[pl.ds(0, nb - 1)], rsem.at[3])
    lane = iota((group, LANES), 1)

    def reduce_half(h):
        mine_rows = pl.ds(h * group, group)
        wait_bytes(recv_l.at[h, pl.ds(0, nb - 1)], rsem.at[12 + h])
        for b in range(blocks):

            def add(r, acc):
                upto = jnp.where(targets[r, place] == b, valid[r, place], 0)
                return acc + jnp.where(lane < upto, recv_l[h, r].astype(F32), 0.0)

            cover = lax.fori_loop(0, nb, add, jnp.zeros((group, LANES), F32), unroll=nb <= 8)
            value = jnp.log(cover + 1.0) - panel[:, pl.ds(b * LANES, LANES)]
            window = pl.ds((b + 1) * LANES, LANES)
            lrx[mine_rows, window] = value
            lh[mine_rows, window], ll[mine_rows, window] = split(value)
        nout[h, 0], nout[h, 1] = pack(lrx.at[mine_rows, :], pair)
        for copy in near[2 * h : 2 * h + 2]:
            copy.start()
        both = mm(
            jnp.concatenate([lh[mine_rows, own], ll[mine_rows, own]], axis=0), kth[...]
        )
        terms = both[:group] + both[group:] + mm(lh[mine_rows, own], ktl[...])
        for c in range(comps // LANES):
            part[pl.ds(h * per_half * rows + c * group, group), :] = terms[
                :, c * LANES : (c + 1) * LANES
            ]

        def spread(hop):
            j = lax.rem(mine + hop, per_half)
            flat = (GROUPS * j + h) * stride
            pl.when(flat != me)(remote(
                part.at[chunk(h, j)], gathered.at[me], 12 + GROUPS + h, dev(flat)
            ).start)

        each(0, per_half, spread)

    for h in range(GROUPS):
        reduce_half(h)


    for copy in w_halo:
        copy.wait_recv()
    none = jnp.zeros((1, bin_dev - LANES), F32)
    to_left = jnp.concatenate([gin[0], none], axis=1)
    to_right = jnp.concatenate([none, gin[1]], axis=1)
    weigh = []
    for row in (own_w[...] + to_left + to_right, to_right, to_left):
        weigh += split(row)
    weigh = jnp.concatenate(
        [piece.astype(F32) for piece in weigh] + [jnp.zeros((10, bin_dev), F32)], axis=0
    ).astype(BF16)

    def weighed(upper, lower):
        return [
            upper[i : i + 1] + upper[i + 1 : i + 2] + lower[i : i + 1] for i in (0, 2, 4)
        ]

    def stacked(l_row, k_row):
        return jnp.concatenate(
            [l_row]
            + [k_row[:, c * LANES : (c + 1) * LANES] for c in range(comps // LANES)]
            + [jnp.zeros((3 - comps // LANES, LANES), F32)],
            axis=0,
        )

    full, over, under = map(
        stacked,
        weighed(mm(weigh, lh[:, own], (1, 1)), mm(weigh, ll[:, own], (1, 1))),
        weighed(mm(weigh, kth[...]), mm(weigh, ktl[...])),
    )
    sums[place] = full
    spill_out[...] = over
    spill = remote(spill_out, spill_in, 1, right)
    spill.start()
    each(1, nb, lambda hop: remote(sums.at[place], sums.at[place], 0, bin_peer(hop)).start())

    def add_and_return(h):
        gathered[me] = part[chunk(h, mine), :]
        wait_bytes(gathered.at[pl.ds(0, ndev - 1)], rsem.at[12 + GROUPS + h])
        c2[chunk(h, mine), :] = jnp.sum(gathered[...], axis=0)
        others(lambda device: remote(
            c2.at[chunk(h, mine)], c2.at[chunk(h, mine)], 12 + 2 * GROUPS + h, device
        ).start())

    for copy in k_halo:
        copy.start()
    pl.when(owner_of(0))(functools.partial(add_and_return, 0))
    pl.when(owner_of(1))(functools.partial(add_and_return, 1))

    for copy in near:
        copy.wait_recv()
    for h in range(GROUPS):
        mine_rows = pl.ds(h * group, group)
        unpack(nin.at[h], lh.at[mine_rows, :], ll.at[mine_rows, :], pair)

    def store_l(m, out):
        smooth_o[:, pl.ds(m * LANES, LANES)] = out

    smooth_first((lh, ll), (ah, al), samples, range(blocks + 1))
    smooth_rest((ah, al), (bh, bl), samples, store_l)

    wait_bytes(sums.at[pl.ds(0, nb - 1)], rsem.at[0])
    totals[seg] = jnp.sum(sums[...], axis=0)
    for hop in range(1, nseg):
        remote(
            totals.at[seg], totals.at[seg], 12 + 3 * GROUPS, (lax.rem(seg + hop, nseg), place)
        ).start()

    def ahead_of(count, mine, ref, mean):
        def earlier(q, acc):
            return acc + jnp.where(q < mine, 1.0, 0.0) * (ref[q] - mean)

        return lax.fori_loop(0, count, earlier, jnp.zeros_like(mean), unroll=count <= 8)

    for copy in k_halo:
        copy.wait_recv()
    unpack(kin, kh, kl, comps // 2)
    smooth_first((kh, kl), (kah, kal), comps, (0, blocks))
    smooth_rest((kah, kal), (bh, bl), comps, store_k)

    spill.wait_recv()
    wait_bytes(totals.at[pl.ds(0, nseg - 1)], rsem.at[12 + 3 * GROUPS])
    mean = jnp.sum(totals[...], axis=0) * (1.0 / ndev)
    before = under - spill_in[...] + ahead_of(nb, place, sums, mean)
    before = before + ahead_of(nseg, seg, totals, mean * nb)
    mean = mean * (1.0 / bin_dev)
    def finish(h):
        mine_rows = pl.ds(h * group, group)
        whole = pl.ds(h * per_half * rows, per_half * rows)
        rest = pl.ds(h * per_half * rows, (per_half - 1) * rows)
        arrived = rsem.at[12 + 2 * GROUPS + h]
        pl.when(owner_of(h))(lambda: wait_bytes(c2.at[rest], arrived))
        pl.when(jnp.logical_not(owner_of(h)))(lambda: wait_bytes(c2.at[whole], arrived))
        coef = jnp.concatenate(
            [
                c2[pl.ds(h * per_half * rows + c * group, group), :]
                for c in range(comps // LANES)
            ],
            axis=1,
        )
        coef_o[mine_rows, :] = coef
        if h < GROUPS - 1:
            combine(
                h, group, total_bins, coef, mean, before, skh, skl,
                smooth_o.at[mine_rows, :], smooth_o.at[mine_rows, :],
                bridge_o.at[mine_rows, :], lambda: None, lambda m: None,
            )

    level_o[:4, :], level_o[4:, :] = mean, before
    for h in range(GROUPS):
        finish(h)

    for h in range(GROUPS):
        wait_bytes(recv_l.at[h, pl.ds(0, nb - 1)], ssem.at[12 + h])
    wait_bytes(targets.at[pl.ds(0, nb - 1)], ssem.at[2])
    wait_bytes(valid.at[pl.ds(0, nb - 1)], ssem.at[3])
    for copy in tap_halo + w_halo + near + k_halo + [spill]:
        copy.wait_send()
    for h in range(GROUPS):
        whole = pl.ds(h * per_half * rows, per_half * rows)
        rest = pl.ds(h * per_half * rows, (per_half - 1) * rows)

        def drain():
            wait_bytes(part.at[rest], ssem.at[12 + GROUPS + h])
            wait_bytes(gathered.at[pl.ds(0, ndev - 1)], ssem.at[12 + 2 * GROUPS + h])

        pl.when(owner_of(h))(drain)
        pl.when(jnp.logical_not(owner_of(h)))(lambda: wait_bytes(part.at[whole], ssem.at[12 + GROUPS + h]))
    wait_bytes(sums.at[pl.ds(0, nb - 1)], ssem.at[0])
    wait_bytes(totals.at[pl.ds(0, nseg - 1)], ssem.at[12 + 3 * GROUPS])


def combine(
    h, group, total_bins, coef, mean, before, skh, skl, smooth_i, smooth_o, bridge_o,
    smooth_done, bridge_done,
):
    comps, bin_dev = skh.shape
    wide = 2 * LANES
    count = bin_dev // wide
    ones = jnp.where(iota((wide, wide), 0) <= iota((wide, wide), 1), 1.0, 0.0).astype(BF16)
    scale = 1.0 / math.sqrt(total_bins)
    eye = iota((group, LANES), 0) + h * group == iota((group, LANES), 1)

    def resolve(level):
        column = jnp.where(eye, level[:1], 0.0)
        for c in range(comps // LANES):
            column = column - coef[:, c * LANES : (c + 1) * LANES] * level[c + 1 : c + 2]
        return jnp.sum(column, axis=1, keepdims=True)

    middle, carry = resolve(mean), resolve(before)
    c_high, c_low = split(coef)
    both = jnp.concatenate([c_high, c_low], axis=0)
    pieces = []
    for m in range(count):
        window = pl.ds(m * wide, wide)
        taken = mm(both, skh[:, window])
        value = smooth_i[:, window] - (
            taken[:group] + taken[group:] + mm(c_high, skl[:, window])
        )
        smooth_o[:, window] = value
        pieces += split(value - middle)
    smooth_done()
    run = mm(jnp.concatenate(pieces, axis=0), ones)
    for m in range(count):
        at = 2 * m * group
        part = run[at : at + group] + run[at + group : at + 2 * group]
        bridge_o[:, pl.ds(m * wide, wide)] = (part + carry) * scale
        carry = carry + part[:, wide - 1 :]
        if m == count // 2 - 1:
            bridge_done(0)
    bridge_done(1)


def close(
    total_bins, coef_i, smooth_i, bridge_i, skh, skl, level,
    coef_o, smooth_o, bridge_o, last_s, last_b, sem,
):
    samples = smooth_i.shape[0]
    group = samples // GROUPS
    middle = smooth_i.shape[1] // 2
    left, right = pl.ds(0, middle), pl.ds(middle, middle)
    ready, last = pl.ds(0, samples - group), pl.ds(samples - group, group)
    copies = [
        pltpu.make_async_copy(smooth_i.at[ready, :], smooth_o.at[ready, :], sem.at[0]),
        pltpu.make_async_copy(bridge_i.at[ready, :], bridge_o.at[ready, :], sem.at[1]),
        pltpu.make_async_copy(coef_i, coef_o, sem.at[2]),
        pltpu.make_async_copy(last_s, smooth_o.at[last, :], sem.at[3]),
        pltpu.make_async_copy(last_b.at[:, left], bridge_o.at[last, left], sem.at[4]),
        pltpu.make_async_copy(last_b.at[:, right], bridge_o.at[last, right], sem.at[5]),
    ]
    for copy in copies[:3]:
        copy.start()
    combine(
        GROUPS - 1, group, total_bins, coef_i[last, :], level[:4, :], level[4:, :], skh, skl,
        smooth_i.at[last, :], last_s, last_b,
        copies[3].start, lambda m: copies[4 + m].start(),
    )
    for copy in copies:
        copy.wait()


def in_hbm(x):
    return pltpu.with_memory_space_constraint(x, pltpu.HBM)


def solution(mesh):
    nseg, nb = mesh.shape["seg"], mesh.shape["bin"]
    ndev = nseg * nb

    def per_device(lanes, targets, valid, panel, comp, kern, starts):
        samples = lanes.shape[1]
        comps, bin_dev = comp.shape
        layers, ntaps = kern.shape[:2]
        ext = bin_dev + 2 * LANES
        flat = samples * comps // LANES
        bands = 3 * (bin_dev // LANES) + 2
        vmem, smem = pltpu.VMEM, pltpu.SMEM
        whole = pl.BlockSpec(memory_space=vmem)
        away = pl.BlockSpec(memory_space=pltpu.HBM)
        sds = jax.ShapeDtypeStruct
        results = (
            sds((samples, comps), F32),
            sds((samples, bin_dev), F32),
            sds((samples, bin_dev), F32),
        )
        found = pl.pallas_call(
            functools.partial(body, nseg, nb),
            out_shape=results + (
                sds((comps, bin_dev), BF16),
                sds((comps, bin_dev), BF16),
                sds((8, LANES), F32),
            ),
            in_specs=[away] * 7,
            out_specs=(whole,) * 6,
            scratch_shapes=[
                smem((nb,) + targets.shape, jnp.int32),
                smem((nb,) + valid.shape, jnp.int32),
                smem(starts.shape, jnp.int32),
                vmem((1, bin_dev), F32),
                vmem((GROUPS, nb, samples // GROUPS, LANES), BF16),
                vmem((comps, ext), F32),
                vmem((layers, ntaps, ext), F32),
                vmem((samples, ext), F32),
                vmem((comps, ext), BF16),
                vmem((comps, ext), BF16),
                vmem((bin_dev, comps), BF16),
                vmem((bin_dev, comps), BF16),
                vmem((samples, ext), BF16),
                vmem((samples, ext), BF16),
                vmem((comps, ext), BF16),
                vmem((comps, ext), BF16),
                vmem((samples, ext), BF16),
                vmem((samples, ext), BF16),
                vmem((comps, ext), BF16),
                vmem((comps, ext), BF16),
                vmem((bands, 2 * LANES, 2 * LANES), BF16),
                vmem((bands, ntaps + 7, LANES), F32),
                vmem((flat, LANES), F32),
                vmem((ndev, max(8, flat // ndev), LANES), F32),
                vmem((flat, LANES), F32),
                vmem((nb, 4, LANES), F32),
                vmem((nseg, 4, LANES), F32),
                vmem((4, LANES), F32),
                vmem((4, LANES), F32),
                vmem((1, bin_dev), F32),
                vmem((2, ntaps, LANES), F32),
                vmem((2, ntaps, LANES), F32),
                vmem((2, 1, LANES), F32),
                vmem((2, 1, LANES), F32),
                vmem((GROUPS, 2, samples // GROUPS // 2, LANES), F32),
                vmem((GROUPS, 2, samples // GROUPS // 2, LANES), F32),
                vmem((2, comps // 2, LANES), F32),
                vmem((2, comps // 2, LANES), F32),
                pltpu.SemaphoreType.DMA((15 + 3 * GROUPS,)),
                pltpu.SemaphoreType.DMA((15 + 3 * GROUPS,)),
                pltpu.SemaphoreType.DMA((6 + GROUPS,)),
            ],
            compiler_params=pltpu.CompilerParams(
                collective_id=0, has_side_effects=True, vmem_limit_bytes=40 << 20
            ),
        )(*map(in_hbm, (targets, valid, starts, lanes, panel.reshape(1, bin_dev), comp, kern)))
        return pl.pallas_call(
            functools.partial(close, bin_dev * ndev),
            out_shape=results,
            in_specs=[whole] * 6,
            out_specs=(away,) * 3,
            scratch_shapes=[
                vmem((samples // GROUPS, bin_dev), F32),
                vmem((samples // GROUPS, bin_dev), F32),
                pltpu.SemaphoreType.DMA((6,)),
            ],
            compiler_params=pltpu.CompilerParams(vmem_limit_bytes=16 << 20),
        )(*found)

    in_specs = (
        P(("seg", "bin"), None, None),
        P(("seg", "bin")),
        P(("seg", "bin")),
        P(("seg", "bin")),
        P(None, ("seg", "bin")),
        P(None, None, ("seg", "bin")),
        P(),
    )
    out_specs = (P(), P(None, ("seg", "bin")), P(None, ("seg", "bin")))
    return jax.shard_map(
        per_device, mesh=mesh, in_specs=in_specs, out_specs=out_specs, check_vma=False
    )
```
